512 devices in a mesh: section: 16 (over x_lo, y, core), seq: 32 (over x_hi, z).
Axes of the slice: x: 4 (x_hi: 2, x_lo: 2; x = x_hi * 2 + x_lo), y: 4, z: 16, core: 2. Of those that a mesh axis runs over, the one named last changes fastest.
Arguments:
- queries: bfloat16 [16, 256, 4096], P('section', 'seq'), may hold values from -110 to 110
- key_value_pages: bfloat16 [16, 64, 4, 2048], P('section', 'seq'), may hold values from -5 to 5
- block_table: int32 [16, 64], replicated, may hold values from 0 to 63, as said below
- page_mask: int32 [16, 1024], replicated, may hold values from 0 to 1, as said below
- noise_level: int32 [16], replicated, may hold values from 0 to 15
- level_gate: float32 [16, 4096], replicated, may hold values from 0.5 to 1.5
Outputs:
- attended: bfloat16 [16, 256, 4096], P('section', 'seq')
The draws below stay inside these ranges and needn't reach their ends.
Inputs may be any that keep to these rules, and one draw needn't show every extreme that they name: `block_table`: each row is a permutation of 0 to 63. `page_mask`: a query span sees all pages of its own span, none of later spans, and some pages of earlier spans.
All inputs are finite; a program needn't handle non-finite values.
Results may differ from the reference program's by a relative error of at most 0.0065.
Values may be sent and summed in bfloat16 or wider, within the bound.
A program may use at most 64 MiB of HBM per device.

```python
import jax
import jax.numpy as jnp
from jax import lax

QUERY_HEADS = 32
KEY_VALUE_HEADS = 8
HEAD_WIDTH = 128
PAGE_TOKENS = 4
LEVELS = 16
VIDEO_SPANS = 16
SPAN_TOKENS = 256
SPAN_PAGES = 64


def shared_pool(key):
    key_value_pool = jax.random.normal(jax.random.fold_in(key, 7), (VIDEO_SPANS, SPAN_PAGES, PAGE_TOKENS, 2 * KEY_VALUE_HEADS * HEAD_WIDTH), jnp.float32)
    key_value_pool = jnp.clip(key_value_pool, -5.0, 5.0)
    return key_value_pool


def shared_tables(key):
    base = jax.random.fold_in(key, 3)
    table = jax.vmap(lambda span: jax.random.permutation(jax.random.fold_in(base, span), SPAN_PAGES))(jnp.arange(VIDEO_SPANS))
    table = table.astype(jnp.int32)
    keep = jax.random.randint(jax.random.fold_in(key, 4), (VIDEO_SPANS, VIDEO_SPANS, SPAN_PAGES), 0, 4) > 0
    query_row = jnp.arange(VIDEO_SPANS)[:, None, None]
    key_span = jnp.arange(VIDEO_SPANS)[None, :, None]
    mask_full = jnp.where(key_span < query_row, keep, key_span == query_row)
    forced = (key_span == 0) & (table[0][None, None, :] <= 1)
    mask_full = (mask_full | forced).astype(jnp.int32).reshape(VIDEO_SPANS, VIDEO_SPANS * SPAN_PAGES)
    return (table, mask_full)


def draw_key_value_pages(key, part):
    return shared_pool(key).astype(jnp.bfloat16)


def draw_block_table(key, part):
    return shared_tables(key)[0]


def draw_page_mask(key, part):
    return shared_tables(key)[1]


def draw_queries(key, part):
    value_rows = jax.random.normal(jax.random.fold_in(key, 5), (VIDEO_SPANS, SPAN_TOKENS, QUERY_HEADS * HEAD_WIDTH), jnp.float32)
    value_rows = jnp.clip(value_rows, -5.0, 5.0)
    value_rows = jnp.clip(value_rows, -110.0, 110.0)
    return value_rows.astype(jnp.bfloat16)


def touch_ends(values, stream_key, smallest, largest):
    shape = values.shape
    spot = [jax.random.randint(jax.random.fold_in(stream_key, axis), (), 0, shape[axis]) for axis in range(len(shape))]
    values = values.at[tuple(spot)].set(smallest)
    longest = shape.index(max(shape))
    spot[longest] = (spot[longest] + 1) % shape[longest]
    return values.at[tuple(spot)].set(largest)


def setup_inputs(seed: int = 0) -> dict:
    streams_of = jax.random.split(jax.random.key(seed), 7)
    queries = draw_queries(jax.random.fold_in(streams_of[6], 71), 0)
    key_value_pages = draw_key_value_pages(jax.random.fold_in(streams_of[6], 71), 0)
    block_table = draw_block_table(jax.random.fold_in(streams_of[6], 71), 0)
    page_mask = draw_page_mask(jax.random.fold_in(streams_of[6], 71), 0)
    noise_level = touch_ends(jax.random.randint(streams_of[4], (VIDEO_SPANS,), 0, LEVELS), jax.random.fold_in(streams_of[4], 1), 0, LEVELS - 1).astype(jnp.int32)
    level_gate = jnp.clip(jax.random.uniform(streams_of[5], (LEVELS, QUERY_HEADS * HEAD_WIDTH), jnp.float32, 0.5, 1.5), 0.5, 1.5)
    return {"queries": queries, "key_value_pages": key_value_pages, "block_table": block_table, "page_mask": page_mask, "noise_level": noise_level, "level_gate": level_gate}


eps = 1e-06

def reference(queries, key_value_pages, block_table, page_mask, noise_level, level_gate):
    span_group = QUERY_HEADS // KEY_VALUE_HEADS
    onehot = (block_table[:, :, None] == jnp.arange(SPAN_PAGES, dtype=jnp.int32)[None, None, :]).astype(jnp.float32)
    logical = page_mask.reshape(VIDEO_SPANS, VIDEO_SPANS, SPAN_PAGES).astype(jnp.float32)
    visible = jnp.einsum('qci,cip->qcp', logical, onehot)
    token_visible = jnp.repeat(visible, PAGE_TOKENS, axis=2).reshape(VIDEO_SPANS, VIDEO_SPANS * SPAN_TOKENS) > 0.5
    gathered_keys = key_value_pages[:, :, :, :KEY_VALUE_HEADS * HEAD_WIDTH].reshape(VIDEO_SPANS * SPAN_TOKENS, KEY_VALUE_HEADS, HEAD_WIDTH)
    gathered_values = key_value_pages[:, :, :, KEY_VALUE_HEADS * HEAD_WIDTH:].reshape(VIDEO_SPANS * SPAN_TOKENS, KEY_VALUE_HEADS, HEAD_WIDTH)
    levels = (noise_level[:, None] == jnp.arange(LEVELS, dtype=jnp.int32)[None, :]).astype(jnp.float32)
    gates = jnp.dot(levels, level_gate, precision=lax.Precision.HIGHEST).reshape(VIDEO_SPANS, QUERY_HEADS, HEAD_WIDTH)
    scale = HEAD_WIDTH ** (-0.5)

    def one_span(span):
        rows = lax.dynamic_index_in_dim(queries, span, 0, keepdims=False).reshape(SPAN_TOKENS, QUERY_HEADS, HEAD_WIDTH)
        seen = lax.dynamic_index_in_dim(token_visible, span, 0, keepdims=False)

        def one_head(head):
            query = lax.dynamic_index_in_dim(rows, head, 1, keepdims=False)
            keys = lax.dynamic_index_in_dim(gathered_keys, head // span_group, 1, keepdims=False)
            value_rows = lax.dynamic_index_in_dim(gathered_values, head // span_group, 1, keepdims=False)
            scores = jnp.dot(query, keys.T, preferred_element_type=jnp.float32) * scale
            scores = jnp.where(seen[None, :], scores, -1e+30)
            top = lax.optimization_barrier(jnp.max(scores, axis=-1, keepdims=True))
            weights = jnp.where(seen[None, :], jnp.exp(scores - top), 0.0)
            total = lax.optimization_barrier(jnp.sum(weights, axis=-1, keepdims=True))
            return jnp.dot(weights.astype(jnp.bfloat16), value_rows, preferred_element_type=jnp.float32) / total
        heads = lax.map(one_head, jnp.arange(QUERY_HEADS, dtype=jnp.int32))
        heads = jnp.transpose(heads, (1, 0, 2))
        normed = heads * lax.rsqrt(lax.optimization_barrier(jnp.mean(heads * heads, axis=-1, keepdims=True)) + eps)
        gate = lax.dynamic_index_in_dim(gates, span, 0, keepdims=False)
        return (normed * gate[None, :, :]).astype(jnp.bfloat16).reshape(SPAN_TOKENS, QUERY_HEADS * HEAD_WIDTH)
    return lax.map(one_span, jnp.arange(VIDEO_SPANS, dtype=jnp.int32))
```

```python
import functools

import jax
import jax.numpy as jnp
from jax import lax
from jax.experimental import pallas as pl
from jax.experimental.pallas import tpu as pltpu
from jax.sharding import PartitionSpec as P

QUERY_HEADS = 32
KEY_VALUE_HEADS = 8
HEAD_WIDTH = 128
SPANS = 16
PAGES = 64
PARTS = 4
PEERS = 8
RUN = 8
GROUP = QUERY_HEADS // KEY_VALUE_HEADS
WIDE = GROUP * HEAD_WIDTH
ROWS = GROUP * PEERS * RUN
SPAN = PARTS * PEERS * RUN
EXPONENT = HEAD_WIDTH ** (-0.5) * 1.4426950408889634
HIDDEN = -3e30
MESH = pl.DeviceIdType.MESH

eps = 1e-06


def kernel(
    queries,
    source,
    table,
    mask,
    noise,
    gates,
    out,
    kv,
    arrived,
    rows,
    ready,
    gate,
    bias,
    top,
    total,
    accum,
    spread_send,
    spread_recv,
    query_send,
    query_recv,
    gate_sem,
    relay_send,
    relay_recv,
    pair_recv,
    out_send,
    out_recv,
):
    s = lax.axis_index("section")
    t = lax.axis_index("seq")
    chip, core = s // 2, s % 2
    x, y = chip // 4, chip % 4
    part = (t % 16) // 4
    me = (t // 16) * 4 + t % 4

    def seat(peer, block):
        return (peer // 4) * 16 + block * 4 + peer % 4

    def section(xx, yy):
        return (xx * 4 + yy) * 2 + core

    up, down = (y + 1) % 4, (y + 3) % 4
    partner = chip * 2 + 1 - core

    barrier = pltpu.get_barrier_semaphore()
    for step in range(1, 32):
        pl.semaphore_signal(barrier, inc=1, device_id=(s, (t + step) % 32), device_id_type=MESH)
    for other in (section(x, up), section(x, down), section(1 - x, y), partner):
        pl.semaphore_signal(barrier, inc=1, device_id=(other, t), device_id_type=MESH)

    gate_copy = pltpu.make_async_copy(
        gates.at[:, pl.ds(pl.multiple_of(me * WIDE, WIDE), WIDE)], gate, gate_sem
    )
    gate_copy.start()

    place = lax.broadcasted_iota(jnp.int32, (SPAN, PAGES), 0)
    holder = ((place // 32) % 2) * 16 + (place // 64) * 4 + (place // 8) % 4
    page = holder * 2 + (place % 8) // 4
    wanted = mask[pl.ds(s, 1), :].astype(jnp.float32)
    for c in range(SPANS):
        onehot = (table[c : c + 1, :] == page).astype(jnp.float32)
        row = jnp.broadcast_to(wanted[:, c * PAGES : (c + 1) * PAGES], (8, PAGES))
        seen = lax.dot_general(row, onehot, (((1,), (1,)), ((), ())))
        bias[c] = jnp.where(seen > 0.5, 0.0, HIDDEN)

    pl.semaphore_wait(barrier, 35)

    sends = []
    local = None
    for turn in (0, 1, 3, 2):
        block = (part + turn) % PARTS
        for step in range(PEERS):
            peer = (me + step) % PEERS
            if turn == 0 and step == 0:
                local = pltpu.make_async_copy(
                    source.at[peer], kv.at[s, part, :, me], spread_recv.at[part]
                )
                local.start()
                continue
            copy = pltpu.make_async_remote_copy(
                src_ref=source.at[peer],
                dst_ref=kv.at[s, part, :, me],
                send_sem=spread_send.at[turn * PEERS + step],
                recv_sem=spread_recv.at[part],
                device_id=(s, seat(peer, block)),
                device_id_type=MESH,
            )
            copy.start()
            sends.append((None, copy))
    for step in range(PEERS):
        peer = (me + step) % PEERS
        piece = queries.at[0, :, pl.ds(pl.multiple_of(peer * WIDE, WIDE), WIDE)]
        if step == 0:
            pltpu.make_async_copy(piece, arrived.at[me], query_recv).start()
            continue
        copy = pltpu.make_async_remote_copy(
            src_ref=piece,
            dst_ref=arrived.at[me],
            send_sem=query_send.at[step],
            recv_sem=query_recv,
            device_id=(s, seat(peer, part)),
            device_id_type=MESH,
        )
        copy.start()
        sends.append((None, copy))

    count = [0]

    def relay(slot, piece, other, condition):
        number = count[0]
        count[0] += 1
        copy = pltpu.make_async_remote_copy(
            src_ref=kv.at[slot, piece],
            dst_ref=kv.at[slot, piece],
            send_sem=relay_send.at[number],
            recv_sem=relay_recv.at[slot, piece],
            device_id=(other, t),
            device_id_type=MESH,
        )

        @pl.when(condition)
        def _():
            copy.start()

        sends.append((condition, copy))

    def share(slot, condition):
        number = count[0]
        count[0] += 1
        copy = pltpu.make_async_remote_copy(
            src_ref=kv.at[slot],
            dst_ref=kv.at[slot],
            send_sem=relay_send.at[number],
            recv_sem=pair_recv.at[slot],
            device_id=(partner, t),
            device_id_type=MESH,
        )

        @pl.when(condition)
        def _():
            copy.start()

        sends.append((condition, copy))

    def landed(slot, piece, condition):
        @pl.when(condition)
        def _():
            pltpu.make_async_copy(
                kv.at[slot, piece], kv.at[slot, piece], relay_recv.at[slot, piece]
            ).wait()

    def shared(slot, condition):
        @pl.when(condition)
        def _():
            pltpu.make_async_copy(kv.at[slot], kv.at[slot], pair_recv.at[slot]).wait()

    def attend(first, spans, condition):
        @pl.when(condition)
        def _():
            keys = jnp.concatenate(
                [kv[first + n, :, 0].reshape(SPAN, HEAD_WIDTH) for n in range(spans)], axis=0
            )
            values = jnp.concatenate(
                [kv[first + n, :, 1].reshape(SPAN, HEAD_WIDTH) for n in range(spans)], axis=0
            )
            hide = jnp.concatenate([bias[first + n, 0:1, :] for n in range(spans)], axis=1)
            scores = lax.dot_general(
                rows[...], keys, (((1,), (1,)), ((), ())), preferred_element_type=jnp.float32
            )
            scores = scores + hide
            before = top[...]
            after = jnp.maximum(before, jnp.max(scores, axis=1, keepdims=True))
            shrink = jnp.exp2((before - after) * EXPONENT)
            weights = jnp.exp2((scores - after) * EXPONENT)
            top[...] = after
            total[...] = total[...] * shrink + jnp.sum(weights, axis=1, keepdims=True)
            accum[...] = accum[...] * shrink + jnp.dot(
                weights.astype(jnp.bfloat16), values, preferred_element_type=jnp.float32
            )

    always = s >= 0
    order = [(part + turn) % PARTS for turn in (0, 1, 3, 2)]

    for piece in order:
        pltpu.make_async_copy(kv.at[s, piece], kv.at[s, piece], spread_recv.at[piece]).wait()
        relay(s, piece, section(x, up), (x == 0) | (y < 3))
        relay(s, piece, section(1, y), x == 0)
        relay(s, piece, section(x, down), y == 0)
    share(s, core == 0)

    pltpu.make_async_copy(arrived, arrived, query_recv).wait()
    for head in range(GROUP):
        lanes = slice(head * HEAD_WIDTH, (head + 1) * HEAD_WIDTH)
        tall = arrived[:, :, lanes].astype(jnp.float32).reshape(PEERS * RUN, HEAD_WIDTH)
        rows[head * PEERS * RUN : (head + 1) * PEERS * RUN, :] = tall.astype(jnp.bfloat16)
    top[...] = jnp.full(top.shape, -1e30, jnp.float32)
    total[...] = jnp.zeros(total.shape, jnp.float32)
    accum[...] = jnp.zeros(accum.shape, jnp.float32)
    attend(s, 1, always)

    chip0 = x * 4 + down
    slot0, gets0, uses0 = chip0 * 2 + core, (x == 0) | (y >= 1), y >= 1
    chip3 = y
    slot3 = chip3 * 2 + core
    far = x == 1
    for piece in order:
        landed(slot0, piece, gets0)
        relay(slot0, piece, section(1, y), x == 0)
        relay(slot0, piece, section(x, up), (y == 1) | (y == 2))
        landed(slot3, piece, far)
        relay(slot3, piece, section(1, down), far)
    share(slot0, uses0)
    share(slot3, far)

    chip4 = down
    slot4 = chip4 * 2 + core
    for piece in order:
        landed(slot4, piece, far)
        relay(slot4, piece, section(1, up), far)
    share(slot4, far)

    shared(chip * 2, core == 1)
    attend(chip * 2, 1, core == 1)

    def take(which, condition):
        shared(which * 2 + 1 - core, condition)
        attend(which * 2, 2, condition)

    def tail(which, condition):
        slot = which * 2 + core
        for piece in order:
            landed(slot, piece, condition)
        share(slot, condition)

    chip1, uses1 = x * 4, y == 3
    chip2, uses2 = x * 4 + (y + 2) % 4, y >= 2
    chip5, chip6 = up, (y + 2) % 4
    take(chip0, uses0)
    tail(chip1, uses1)
    tail(chip2, uses2)
    take(chip3, far)
    tail(chip5, far)
    take(chip1, uses1)
    take(chip2, uses2)
    take(chip4, far)
    tail(chip6, far)
    take(chip5, far)
    take(chip6, far)

    gate_copy.wait()
    level = noise[s]
    row = gate[pl.ds(level, 1), :]
    mixed = accum[...] / total[...]
    normed = mixed * lax.rsqrt(jnp.mean(mixed * mixed, axis=1, keepdims=True) + eps)
    for head in range(GROUP):
        lanes = slice(head * HEAD_WIDTH, (head + 1) * HEAD_WIDTH)
        block = normed[head * PEERS * RUN : (head + 1) * PEERS * RUN, :] * row[:, lanes]
        ready[:, :, lanes] = block.reshape(PEERS, RUN, HEAD_WIDTH).astype(jnp.bfloat16)
    mine = out.at[0, :, pl.ds(pl.multiple_of(me * WIDE, WIDE), WIDE)]
    for step in range(PEERS):
        peer = (me + step) % PEERS
        if step == 0:
            pltpu.make_async_copy(ready.at[peer], mine, out_recv).start()
            continue
        copy = pltpu.make_async_remote_copy(
            src_ref=ready.at[peer],
            dst_ref=mine,
            send_sem=out_send.at[step],
            recv_sem=out_recv,
            device_id=(s, seat(peer, part)),
            device_id_type=MESH,
        )
        copy.start()
        sends.append((None, copy))

    for condition, copy in sends:
        if condition is None:
            copy.wait_send()
        else:
            pl.when(condition)(copy.wait_send)
    pltpu.make_async_copy(out, out, out_recv).wait()


def body(queries, key_value_pages, block_table, page_mask, noise_level, level_gate):
    source = key_value_pages.reshape(RUN, 2, KEY_VALUE_HEADS, HEAD_WIDTH).transpose(2, 1, 0, 3)
    vmem = pl.BlockSpec(memory_space=pltpu.VMEM)
    anywhere = pl.BlockSpec(memory_space=pl.ANY)
    dma = pltpu.SemaphoreType.DMA
    return pl.pallas_call(
        kernel,
        out_shape=jax.ShapeDtypeStruct(queries.shape, jnp.bfloat16),
        in_specs=[
            anywhere,
            anywhere,
            vmem,
            vmem,
            pl.BlockSpec(memory_space=pltpu.SMEM),
            anywhere,
        ],
        out_specs=vmem,
        scratch_shapes=[
            pltpu.VMEM((SPANS, PARTS, 2, PEERS, RUN, HEAD_WIDTH), jnp.bfloat16),
            pltpu.VMEM((PEERS, RUN, WIDE), jnp.bfloat16),
            pltpu.VMEM((ROWS, HEAD_WIDTH), jnp.bfloat16),
            pltpu.VMEM((PEERS, RUN, WIDE), jnp.bfloat16),
            pltpu.VMEM((level_gate.shape[0], WIDE), jnp.float32),
            pltpu.VMEM((SPANS, 8, SPAN), jnp.float32),
            pltpu.VMEM((ROWS, 1), jnp.float32),
            pltpu.VMEM((ROWS, 1), jnp.float32),
            pltpu.VMEM((ROWS, HEAD_WIDTH), jnp.float32),
            dma((32,)),
            dma((PARTS,)),
            dma((PEERS,)),
            dma,
            dma,
            dma((64,)),
            dma((SPANS, PARTS)),
            dma((SPANS,)),
            dma((PEERS,)),
            dma,
        ],
        compiler_params=pltpu.CompilerParams(collective_id=0, has_side_effects=True),
    )(queries, source, block_table, page_mask, noise_level, level_gate)


def solution(mesh):
    in_specs = (P("section", "seq", None), P("section", "seq", None, None), P(), P(), P(), P())
    out_specs = P("section", "seq", None)
    return jax.shard_map(body, mesh=mesh, in_specs=in_specs, out_specs=out_specs, check_vma=False)
```

```python
import functools

import jax
import jax.numpy as jnp
from jax import lax
from jax.experimental import pallas as pl
from jax.experimental.pallas import tpu as pltpu
from jax.sharding import PartitionSpec as P

QUERY_HEADS = 32
KEY_VALUE_HEADS = 8
HEAD_WIDTH = 128
SPANS = 16
PAGES = 64
PARTS = 4
PEERS = 8
RUN = 8
GROUP = QUERY_HEADS // KEY_VALUE_HEADS
WIDE = GROUP * HEAD_WIDTH
ROWS = GROUP * PEERS * RUN
SPAN = PARTS * PEERS * RUN
EXPONENT = HEAD_WIDTH ** (-0.5) * 1.4426950408889634
HIDDEN = -3e30
MESH = pl.DeviceIdType.MESH

eps = 1e-06


def kernel(
    queries,
    pool,
    table_any,
    mask_any,
    noise,
    gates,
    out,
    kv,
    arrived,
    rows,
    ready,
    gate,
    raw,
    source,
    table,
    mask,
    bias,
    top,
    total,
    accum,
    local_sem,
    spread_send,
    spread_recv,
    query_send,
    query_recv,
    deep_send,
    deep_recv,
    half_recv,
    relay_send,
    relay_recv,
    share_send,
    share_recv,
    out_send,
    out_recv,
):
    s = lax.axis_index("section")
    t = lax.axis_index("seq")
    chip, core = s // 2, s % 2
    x, y = chip // 4, chip % 4
    column, z = t // 16, t % 16
    part = z // 4
    me = column * 4 + z % 4

    def seat(peer):
        return (peer // 4) * 16 + part * 4 + peer % 4

    def section(xx, yy):
        return (xx * 4 + yy) * 2 + core

    up, down = (y + 1) % 4, (y + 3) % 4
    partner = chip * 2 + 1 - core
    ahead, behind = column * 16 + (z + 4) % 16, column * 16 + (z + 12) % 16

    barrier = pltpu.get_barrier_semaphore()
    near = [(s, seat((me + step) % PEERS)) for step in range(1, PEERS)]
    near += [(s, ahead), (s, behind)]
    near += [(other, t) for other in (section(x, up), section(x, down), section(1 - x, y), partner)]
    for other in near:
        pl.semaphore_signal(barrier, inc=1, device_id=other, device_id_type=MESH)

    mine = pl.ds(pl.multiple_of(me * WIDE, WIDE), WIDE)
    loads = [
        pltpu.make_async_copy(pool.at[0], raw, local_sem.at[0]),
        pltpu.make_async_copy(table_any, table, local_sem.at[1]),
        pltpu.make_async_copy(mask_any, mask, local_sem.at[2]),
        pltpu.make_async_copy(gates.at[:, mine], gate, local_sem.at[3]),
    ]
    for load in loads:
        load.start()

    loads[0].wait()
    for head in range(KEY_VALUE_HEADS):
        for kind in range(2):
            first = (kind * KEY_VALUE_HEADS + head) * HEAD_WIDTH
            for page in range(2):
                source[head, kind, page * 4 : (page + 1) * 4, :] = raw[
                    page, :, first : first + HEAD_WIDTH
                ]

    @pl.when(core == 0)
    def _():
        kv[s + 1] = jnp.zeros(kv.shape[1:], kv.dtype)

    top[...] = jnp.full(top.shape, -1e30, jnp.float32)
    total[...] = jnp.zeros(total.shape, jnp.float32)
    accum[...] = jnp.zeros(accum.shape, jnp.float32)

    pl.semaphore_wait(barrier, len(near))

    sends = []
    pltpu.make_async_copy(source.at[me], kv.at[s, part, :, me], spread_recv).start()
    for step in range(1, PEERS):
        peer = (me + step) % PEERS
        copy = pltpu.make_async_remote_copy(
            src_ref=source.at[peer],
            dst_ref=kv.at[s, part, :, me],
            send_sem=spread_send.at[step],
            recv_sem=spread_recv,
            device_id=(s, seat(peer)),
            device_id_type=MESH,
        )
        copy.start()
        sends.append((None, copy))
    for step in range(PEERS):
        peer = (me + step) % PEERS
        piece = queries.at[0, :, pl.ds(pl.multiple_of(peer * WIDE, WIDE), WIDE)]
        if step == 0:
            pltpu.make_async_copy(piece, arrived.at[me], query_recv).start()
            continue
        copy = pltpu.make_async_remote_copy(
            src_ref=piece,
            dst_ref=arrived.at[me],
            send_sem=query_send.at[step],
            recv_sem=query_recv,
            device_id=(s, seat(peer)),
            device_id_type=MESH,
        )
        copy.start()
        sends.append((None, copy))

    loads[1].wait()
    loads[2].wait()
    place = lax.broadcasted_iota(jnp.int32, (SPAN, PAGES), 0)
    holder = ((place // 32) % 2) * 16 + (place // 64) * 4 + (place // 8) % 4
    page = holder * 2 + (place % 8) // 4
    wanted = mask[pl.ds(s, 1), :].astype(jnp.float32)
    for c in range(SPANS):
        onehot = (table[c : c + 1, :] == page).astype(jnp.float32)
        row = jnp.broadcast_to(wanted[:, c * PAGES : (c + 1) * PAGES], (8, PAGES))
        seen = lax.dot_general(row, onehot, (((1,), (1,)), ((), ())))
        hide = jnp.where(seen > 0.5, 0.0, HIDDEN)
        lanes = slice((c % 2) * 64, (c % 2) * 64 + 64)
        for piece in range(PARTS):
            bias[c // 2, piece, :, lanes] = hide[:, piece * 64 : (piece + 1) * 64]

    def deep(src, number, arrival, other):
        copy = pltpu.make_async_remote_copy(
            src_ref=src,
            dst_ref=src,
            send_sem=deep_send.at[number],
            recv_sem=arrival,
            device_id=(s, other),
            device_id_type=MESH,
        )
        copy.start()
        sends.append((None, copy))

    count = [0, 0]

    def relay(slot, piece, other, condition):
        copy = pltpu.make_async_remote_copy(
            src_ref=kv.at[slot, piece],
            dst_ref=kv.at[slot, piece],
            send_sem=relay_send.at[count[0]],
            recv_sem=relay_recv.at[slot, piece],
            device_id=(other, t),
            device_id_type=MESH,
        )
        count[0] += 1
        pl.when(condition)(copy.start)
        sends.append((condition, copy))

    def share(slot, piece, condition):
        copy = pltpu.make_async_remote_copy(
            src_ref=kv.at[slot, piece],
            dst_ref=kv.at[slot, piece],
            send_sem=share_send.at[count[1]],
            recv_sem=share_recv.at[slot, piece],
            device_id=(partner, t),
            device_id_type=MESH,
        )
        count[1] += 1
        pl.when(condition)(copy.start)
        sends.append((condition, copy))

    def arrival(ref, sem):
        pltpu.make_async_copy(ref, ref, sem).wait()

    def landed(slot, piece, condition):
        @pl.when(condition)
        def _():
            arrival(kv.at[slot, piece], relay_recv.at[slot, piece])

    def attend(which, pieces, condition):
        @pl.when(condition)
        def _():
            units = [(which * 2 + n, piece) for piece in pieces for n in range(2)]
            keys, values = (
                jnp.concatenate(
                    [kv[a, b, kind].reshape(PEERS * RUN, HEAD_WIDTH) for a, b in units], axis=0
                )
                for kind in range(2)
            )
            hide = jnp.concatenate([bias[which, piece, 0:1, :] for piece in pieces], axis=1)
            scores = lax.dot_general(
                rows[...], keys, (((1,), (1,)), ((), ())), preferred_element_type=jnp.float32
            )
            scores = scores + hide
            before = top[...]
            after = jnp.maximum(before, jnp.max(scores, axis=1, keepdims=True))
            shrink = jnp.exp2((before - after) * EXPONENT)
            weights = jnp.exp2((scores - after) * EXPONENT)
            top[...] = after
            total[...] = total[...] * shrink + jnp.sum(weights, axis=1, keepdims=True)
            accum[...] = accum[...] * shrink + jnp.dot(
                weights.astype(jnp.bfloat16), values, preferred_element_type=jnp.float32
            )

    always = s >= 0
    far = x == 1
    first, after1, before1, opposite = (part + 0, (part + 1) % 4, (part + 3) % 4, (part + 2) % 4)

    def outward(piece):
        relay(s, piece, section(x, up), (x == 0) | (y < 3))
        relay(s, piece, section(1, y), x == 0)
        relay(s, piece, section(x, down), y == 0)
        share(s, piece, core == 0)

    chip0, chip1, chip2 = x * 4 + down, x * 4, x * 4 + (y + 2) % 4
    chip3, chip4, chip5, chip6 = y, down, up, (y + 2) % 4
    gets0, uses0, uses1, uses2 = (x == 0) | (y >= 1), y >= 1, y == 3, y >= 2

    def early(piece):
        slot = chip0 * 2 + core
        landed(slot, piece, gets0)
        relay(slot, piece, section(1, y), x == 0)
        relay(slot, piece, section(x, up), (y == 1) | (y == 2))
        share(slot, piece, uses0)
        slot = chip3 * 2 + core
        landed(slot, piece, far)
        relay(slot, piece, section(1, down), far)
        share(slot, piece, far)

    def middle(piece):
        slot = chip4 * 2 + core
        landed(slot, piece, far)
        relay(slot, piece, section(1, up), far)
        share(slot, piece, far)

    def late(piece, which, condition):
        slot = which * 2 + core
        landed(slot, piece, condition)
        share(slot, piece, condition)

    def tail(piece):
        late(piece, chip1, uses1)
        late(piece, chip2, uses2)
        late(piece, chip5, far)
        late(piece, chip6, far)

    def take(which, pieces, condition):
        slot = which * 2 + 1 - core
        for piece in pieces:

            @pl.when(condition)
            def _():
                arrival(kv.at[slot, piece], share_recv.at[slot, piece])

        attend(which, pieces, condition)

    def own(pieces):
        for piece in pieces:

            @pl.when(core == 1)
            def _():
                arrival(kv.at[chip * 2, piece], share_recv.at[chip * 2, piece])

        attend(chip, pieces, always)

    arrival(kv.at[s, first], spread_recv)
    deep(kv.at[s, first], 0, deep_recv.at[0], ahead)
    deep(kv.at[s, first], 1, deep_recv.at[1], behind)
    outward(first)

    arrival(arrived, query_recv)
    for head in range(GROUP):
        lanes = slice(head * HEAD_WIDTH, (head + 1) * HEAD_WIDTH)
        tall = arrived[:, :, lanes].astype(jnp.float32).reshape(PEERS * RUN, HEAD_WIDTH)
        rows[head * PEERS * RUN : (head + 1) * PEERS * RUN, :] = tall.astype(jnp.bfloat16)

    early(first)
    arrival(kv.at[s, before1], deep_recv.at[0])
    deep(kv.at[s, before1, 0], 2, half_recv.at[0], ahead)
    outward(before1)
    arrival(kv.at[s, after1], deep_recv.at[1])
    deep(kv.at[s, after1, 1], 3, half_recv.at[1], behind)
    outward(after1)
    middle(first)
    early(before1)
    early(after1)
    arrival(kv.at[s, opposite, 0], half_recv.at[0])
    arrival(kv.at[s, opposite, 1], half_recv.at[1])
    outward(opposite)
    middle(before1)
    middle(after1)
    tail(first)
    early(opposite)
    most = (first, before1, after1)
    own(most)
    take(chip0, most, uses0)
    middle(opposite)
    tail(before1)
    tail(after1)
    take(chip3, most, far)
    take(chip4, most, far)
    take(chip1, most, uses1)
    take(chip2, most, uses2)
    take(chip5, most, far)
    take(chip6, most, far)
    last = (opposite,)
    tail(opposite)
    own(last)
    take(chip0, last, uses0)
    take(chip3, last, far)
    take(chip4, last, far)
    take(chip1, last, uses1)
    take(chip2, last, uses2)
    take(chip5, last, far)
    take(chip6, last, far)

    loads[3].wait()
    level = noise[s]
    row = gate[pl.ds(level, 1), :]
    mixed = accum[...] / total[...]
    normed = mixed * lax.rsqrt(jnp.mean(mixed * mixed, axis=1, keepdims=True) + eps)
    for head in range(GROUP):
        lanes = slice(head * HEAD_WIDTH, (head + 1) * HEAD_WIDTH)
        block = normed[head * PEERS * RUN : (head + 1) * PEERS * RUN, :] * row[:, lanes]
        ready[:, :, lanes] = block.reshape(PEERS, RUN, HEAD_WIDTH).astype(jnp.bfloat16)
    pltpu.make_async_copy(ready.at[me], out.at[0, :, mine], out_recv).start()
    for step in range(1, PEERS):
        peer = (me + step) % PEERS
        copy = pltpu.make_async_remote_copy(
            src_ref=ready.at[peer],
            dst_ref=out.at[0, :, mine],
            send_sem=out_send.at[step],
            recv_sem=out_recv,
            device_id=(s, seat(peer)),
            device_id_type=MESH,
        )
        copy.start()
        sends.append((None, copy))

    for condition, copy in sends:
        if condition is None:
            copy.wait_send()
        else:
            pl.when(condition)(copy.wait_send)
    arrival(out, out_recv)


def body(queries, key_value_pages, block_table, page_mask, noise_level, level_gate):
    anywhere = pl.BlockSpec(memory_space=pl.ANY)
    dma = pltpu.SemaphoreType.DMA
    return pl.pallas_call(
        kernel,
        out_shape=jax.ShapeDtypeStruct(queries.shape, jnp.bfloat16),
        in_specs=[
            anywhere,
            anywhere,
            anywhere,
            anywhere,
            pl.BlockSpec(memory_space=pltpu.SMEM),
            anywhere,
        ],
        out_specs=anywhere,
        scratch_shapes=[
            pltpu.VMEM((SPANS, PARTS, 2, PEERS, RUN, HEAD_WIDTH), jnp.bfloat16),
            pltpu.VMEM((PEERS, RUN, WIDE), jnp.bfloat16),
            pltpu.VMEM((ROWS, HEAD_WIDTH), jnp.bfloat16),
            pltpu.VMEM((PEERS, RUN, WIDE), jnp.bfloat16),
            pltpu.VMEM((level_gate.shape[0], WIDE), jnp.float32),
            pltpu.VMEM(key_value_pages.shape[1:], jnp.bfloat16),
            pltpu.VMEM((KEY_VALUE_HEADS, 2, RUN, HEAD_WIDTH), jnp.bfloat16),
            pltpu.VMEM(block_table.shape, jnp.int32),
            pltpu.VMEM(page_mask.shape, jnp.int32),
            pltpu.VMEM((SPANS // 2, PARTS, 8, 128), jnp.float32),
            pltpu.VMEM((ROWS, 1), jnp.float32),
            pltpu.VMEM((ROWS, 1), jnp.float32),
            pltpu.VMEM((ROWS, HEAD_WIDTH), jnp.float32),
            dma((4,)),
            dma((PEERS,)),
            dma,
            dma((PEERS,)),
            dma,
            dma((4,)),
            dma((2,)),
            dma((2,)),
            dma((32,)),
            dma((SPANS, PARTS)),
            dma((32,)),
            dma((SPANS, PARTS)),
            dma((PEERS,)),
            dma,
        ],
        compiler_params=pltpu.CompilerParams(collective_id=0, has_side_effects=True),
    )(queries, key_value_pages, block_table, page_mask, noise_level, level_gate)


def solution(mesh):
    in_specs = (P("section", "seq", None), P("section", "seq", None, None), P(), P(), P(), P())
    out_specs = P("section", "seq", None)
    return jax.shard_map(body, mesh=mesh, in_specs=in_specs, out_specs=out_specs, check_vma=False)
```

```python
import functools

import jax
import jax.numpy as jnp
from jax import lax
from jax.experimental import pallas as pl
from jax.experimental.pallas import tpu as pltpu
from jax.sharding import PartitionSpec as P

QUERY_HEADS = 32
KEY_VALUE_HEADS = 8
HEAD_WIDTH = 128
SPANS = 16
PAGES = 64
PARTS = 4
PEERS = 8
RUN = 8
GROUP = QUERY_HEADS // KEY_VALUE_HEADS
WIDE = GROUP * HEAD_WIDTH
ROWS = GROUP * PEERS * RUN
SPAN = PARTS * PEERS * RUN
EXPONENT = HEAD_WIDTH ** (-0.5) * 1.4426950408889634
HIDDEN = -3e30
MESH = pl.DeviceIdType.MESH

eps = 1e-06


def kernel(
    queries,
    pool,
    table_any,
    mask_any,
    noise_any,
    gates,
    out,
    kv,
    arrived,
    rows,
    ready,
    gate,
    raw,
    source,
    table,
    mask,
    noise,
    bias,
    top,
    total,
    accum,
    local_sem,
    spread_send,
    spread_recv,
    deep_send,
    query_send,
    query_recv,
    relay_send,
    relay_recv,
    share_send,
    share_recv,
    out_send,
    out_recv,
):
    s = lax.axis_index("section")
    t = lax.axis_index("seq")
    chip, core = s // 2, s % 2
    x, y = chip // 4, chip % 4
    column, z = t // 16, t % 16
    part = z // 4
    me = column * 4 + z % 4
    ahead, behind = column * 16 + (z + 4) % 16, column * 16 + (z + 12) % 16

    def seat(peer, block):
        return (peer // 4) * 16 + block * 4 + peer % 4

    def section(xx, yy):
        return (xx * 4 + yy) * 2 + core

    up, down = (y + 1) % 4, (y + 3) % 4
    partner = chip * 2 + 1 - core

    barrier = pltpu.get_barrier_semaphore()
    corner = section(1 - x, (y + 1 + 2 * x) % 4)
    for other in (section(x, up), section(x, down), section(1 - x, y), corner, partner):
        pl.semaphore_signal(barrier, inc=1, device_id=(other, t), device_id_type=MESH)
    for step in range(1, PEERS):
        pl.semaphore_signal(
            barrier, inc=1, device_id=(s, seat((me + step) % PEERS, part)), device_id_type=MESH
        )
    for block in range(1, PARTS):

        @pl.when((part < block) & (part < 2))
        def _():
            for peer in range(PEERS):
                pl.semaphore_signal(
                    barrier, inc=1, device_id=(s, seat(peer, block)), device_id_type=MESH
                )

    @pl.when(part >= 2)
    def _():
        pl.semaphore_signal(
            barrier,
            inc=1,
            device_id=(s, column * 16 + (z + 4 * (5 - 2 * part) + 32) % 16),
            device_id_type=MESH,
        )

    mine = pl.ds(pl.multiple_of(me * WIDE, WIDE), WIDE)
    loads = [
        pltpu.make_async_copy(pool.at[0], raw, local_sem.at[0]),
        pltpu.make_async_copy(table_any, table, local_sem.at[1]),
        pltpu.make_async_copy(mask_any, mask, local_sem.at[2]),
        pltpu.make_async_copy(gates.at[:, mine], gate, local_sem.at[3]),
        pltpu.make_async_copy(noise_any, noise, local_sem.at[4]),
    ]
    for load in loads:
        load.start()

    loads[0].wait()
    for head in range(KEY_VALUE_HEADS):
        for kind in range(2):
            first = (kind * KEY_VALUE_HEADS + head) * HEAD_WIDTH
            for page in range(2):
                source[head, kind, page * 4 : (page + 1) * 4, :] = raw[
                    page, :, first : first + HEAD_WIDTH
                ]

    @pl.when(core == 0)
    def _():
        kv[s + 1] = jnp.zeros(kv.shape[1:], kv.dtype)

    top[...] = jnp.full(top.shape, -1e30, jnp.float32)
    total[...] = jnp.zeros(total.shape, jnp.float32)
    accum[...] = jnp.zeros(accum.shape, jnp.float32)

    low = part < 2
    lower = jnp.minimum(part, 2)
    pl.semaphore_wait(barrier, 12 + PEERS * lower + jnp.where(low, 0, 1))

    sends = []

    def spread(turn, step, block, condition):
        peer = (me + step) % PEERS
        copy = pltpu.make_async_remote_copy(
            src_ref=source.at[peer],
            dst_ref=kv.at[s, part, :, me],
            send_sem=spread_send.at[turn * PEERS + step],
            recv_sem=spread_recv.at[part],
            device_id=(s, seat(peer, block)),
            device_id_type=MESH,
        )
        pl.when(condition)(copy.start)
        sends.append((condition, copy))

    for block in range(2):
        for step in range(PEERS):
            spread(block + 1, step, block, block < lower)
    pltpu.make_async_copy(source.at[me], kv.at[s, part, :, me], spread_recv.at[part]).start()
    for step in range(1, PEERS):
        spread(0, step, part, s >= 0)
    for step in range(PEERS):
        peer = (me + step) % PEERS
        piece = queries.at[0, :, pl.ds(pl.multiple_of(peer * WIDE, WIDE), WIDE)]
        if step == 0:
            pltpu.make_async_copy(piece, arrived.at[me], query_recv).start()
            continue
        copy = pltpu.make_async_remote_copy(
            src_ref=piece,
            dst_ref=arrived.at[me],
            send_sem=query_send.at[step],
            recv_sem=query_recv,
            device_id=(s, seat(peer, part)),
            device_id_type=MESH,
        )
        copy.start()
        sends.append((None, copy))

    loads[1].wait()
    loads[2].wait()
    place = lax.broadcasted_iota(jnp.int32, (SPAN, PAGES), 0)
    holder = ((place // 32) % 2) * 16 + (place // 64) * 4 + (place // 8) % 4
    page = holder * 2 + (place % 8) // 4
    wanted = mask[pl.ds(s, 1), :].astype(jnp.float32)
    for c in range(SPANS):
        onehot = (table[c : c + 1, :] == page).astype(jnp.float32)
        row = jnp.broadcast_to(wanted[:, c * PAGES : (c + 1) * PAGES], (8, PAGES))
        seen = lax.dot_general(row, onehot, (((1,), (1,)), ((), ())))
        hide = jnp.where(seen > 0.5, 0.0, HIDDEN)
        lanes = slice((c % 2) * 64, (c % 2) * 64 + 64)
        for piece in range(PARTS):
            bias[c // 2, piece, :, lanes] = hide[:, piece * 64 : (piece + 1) * 64]

    count = [0, 0]

    def relay(slot, piece, other, condition):
        copy = pltpu.make_async_remote_copy(
            src_ref=kv.at[slot, piece],
            dst_ref=kv.at[slot, piece],
            send_sem=relay_send.at[count[0]],
            recv_sem=relay_recv.at[slot, piece],
            device_id=(other, t),
            device_id_type=MESH,
        )
        count[0] += 1
        pl.when(condition)(copy.start)
        sends.append((condition, copy))

    def share(slot, piece, condition):
        copy = pltpu.make_async_remote_copy(
            src_ref=kv.at[slot, piece],
            dst_ref=kv.at[slot, piece],
            send_sem=share_send.at[count[1]],
            recv_sem=share_recv.at[slot, piece],
            device_id=(partner, t),
            device_id_type=MESH,
        )
        count[1] += 1
        pl.when(condition)(copy.start)
        sends.append((condition, copy))

    def arrival(ref, sem):
        pltpu.make_async_copy(ref, ref, sem).wait()

    def landed(slot, piece, condition):
        @pl.when(condition)
        def _():
            arrival(kv.at[slot, piece], relay_recv.at[slot, piece])

    def attend(which, pieces, condition):
        @pl.when(condition)
        def _():
            units = [(which * 2 + n, piece) for piece in pieces for n in range(2)]
            keys, values = (
                jnp.concatenate(
                    [kv[a, b, kind].reshape(PEERS * RUN, HEAD_WIDTH) for a, b in units], axis=0
                )
                for kind in range(2)
            )
            hide = jnp.concatenate([bias[which, piece, 0:1, :] for piece in pieces], axis=1)
            scores = lax.dot_general(
                rows[...], keys, (((1,), (1,)), ((), ())), preferred_element_type=jnp.float32
            )
            scores = scores + hide
            before = top[...]
            after = jnp.maximum(before, jnp.max(scores, axis=1, keepdims=True))
            shrink = jnp.exp2((before - after) * EXPONENT)
            weights = jnp.exp2((scores - after) * EXPONENT)
            top[...] = after
            total[...] = total[...] * shrink + jnp.sum(weights, axis=1, keepdims=True)
            accum[...] = accum[...] * shrink + jnp.dot(
                weights.astype(jnp.bfloat16), values, preferred_element_type=jnp.float32
            )

    always = s >= 0
    far = x == 1

    others = [part, (part + 1) % 4, (part + 2) % 4, (part + 3) % 4]
    for turn in range(1, PARTS):
        others[turn] = jnp.where(part == 3, (turn + 1) % 3, others[turn])

    def deep(number, piece, other, condition):
        copy = pltpu.make_async_remote_copy(
            src_ref=kv.at[s, piece],
            dst_ref=kv.at[s, piece],
            send_sem=deep_send.at[number],
            recv_sem=spread_recv.at[piece],
            device_id=(s, other),
            device_id_type=MESH,
        )
        pl.when(condition)(copy.start)
        sends.append((condition, copy))

    def collect(turn):
        piece = others[turn]
        arrival(kv.at[s, piece], spread_recv.at[piece])
        outward(piece)
        if turn == 0:
            deep(0, part, column * 16 + (z + 4 * (5 - 2 * part) + 32) % 16, part >= 2)
        if turn == 1:
            deep(1, part, ahead, part < 2)
        if turn == 3:
            deep(2, part, behind, part == 0)
            deep(3, others[1], behind, part == 0)
            deep(4, piece, ahead, part == 1)

    def outward(piece):
        relay(s, piece, section(x, up), (x == 0) | (y < 3))
        relay(s, piece, section(1, y), x == 0)
        relay(s, piece, section(x, down), y == 0)
        share(s, piece, core == 0)

    chip0, chip1, chip2 = x * 4 + down, x * 4, x * 4 + (y + 2) % 4
    chip3, chip4, chip5, chip6 = y, down, up, (y + 2) % 4
    gets0, uses0, uses1, uses2 = (x == 0) | (y >= 1), y >= 1, y == 3, y >= 2

    def early(piece):
        slot = chip0 * 2 + core
        landed(slot, piece, gets0)
        relay(slot, piece, section(1, y), x == 0)
        relay(slot, piece, section(x, up), (y == 1) | (y == 2))
        relay(slot, piece, section(1, up), x == 0)
        share(slot, piece, uses0)
        slot = chip3 * 2 + core
        landed(slot, piece, far)
        relay(slot, piece, section(1, down), far)
        share(slot, piece, far)

    def late(piece, which, condition):
        slot = which * 2 + core
        landed(slot, piece, condition)
        share(slot, piece, condition)

    def tail(piece):
        late(piece, chip4, far)
        late(piece, chip1, uses1)
        late(piece, chip2, uses2)
        late(piece, chip5, far)
        late(piece, chip6, far)

    def take(which, pieces, condition):
        slot = which * 2 + 1 - core
        for piece in pieces:

            @pl.when(condition)
            def _():
                arrival(kv.at[slot, piece], share_recv.at[slot, piece])

        attend(which, pieces, condition)

    def own(pieces):
        for piece in pieces:

            @pl.when(core == 1)
            def _():
                arrival(kv.at[chip * 2, piece], share_recv.at[chip * 2, piece])

        attend(chip, pieces, always)

    collect(0)
    arrival(arrived, query_recv)
    for head in range(GROUP):
        lanes = slice(head * HEAD_WIDTH, (head + 1) * HEAD_WIDTH)
        tall = arrived[:, :, lanes].astype(jnp.float32).reshape(PEERS * RUN, HEAD_WIDTH)
        rows[head * PEERS * RUN : (head + 1) * PEERS * RUN, :] = tall.astype(jnp.bfloat16)

    part0, part1, part2, part3 = others
    half, rest = (part0, part1), (part2, part3)
    early(part0)
    collect(1)
    tail(part0)
    early(part1)
    collect(2)
    collect(3)
    own(half)
    take(chip0, half, uses0)
    take(chip3, half, far)
    early(part2)
    early(part3)
    tail(part1)
    take(chip4, half, far)
    take(chip1, half, uses1)
    take(chip2, half, uses2)
    take(chip5, half, far)
    take(chip6, half, far)
    own(rest)
    tail(part2)
    tail(part3)
    take(chip0, rest, uses0)
    take(chip3, rest, far)
    take(chip4, rest, far)
    take(chip1, rest, uses1)
    take(chip2, rest, uses2)
    take(chip5, rest, far)
    take(chip6, rest, far)

    loads[3].wait()
    loads[4].wait()
    level = noise[s]
    row = gate[pl.ds(level, 1), :]
    mixed = accum[...] / total[...]
    normed = mixed * lax.rsqrt(jnp.mean(mixed * mixed, axis=1, keepdims=True) + eps)
    for head in range(GROUP):
        lanes = slice(head * HEAD_WIDTH, (head + 1) * HEAD_WIDTH)
        block = normed[head * PEERS * RUN : (head + 1) * PEERS * RUN, :] * row[:, lanes]
        ready[:, :, lanes] = block.reshape(PEERS, RUN, HEAD_WIDTH).astype(jnp.bfloat16)
    pltpu.make_async_copy(ready.at[me], out.at[0, :, mine], out_recv).start()
    for step in range(1, PEERS):
        peer = (me + step) % PEERS
        copy = pltpu.make_async_remote_copy(
            src_ref=ready.at[peer],
            dst_ref=out.at[0, :, mine],
            send_sem=out_send.at[step],
            recv_sem=out_recv,
            device_id=(s, seat(peer, part)),
            device_id_type=MESH,
        )
        copy.start()
        sends.append((None, copy))

    for condition, copy in sends:
        if condition is None:
            copy.wait_send()
        else:
            pl.when(condition)(copy.wait_send)
    arrival(out, out_recv)


def body(*arrays):
    queries, key_value_pages, block_table, page_mask, noise_level, level_gate = arrays
    anywhere = pl.BlockSpec(memory_space=pl.ANY)
    dma = pltpu.SemaphoreType.DMA
    return pl.pallas_call(
        kernel,
        out_shape=jax.ShapeDtypeStruct(queries.shape, jnp.bfloat16),
        in_specs=[anywhere] * len(arrays),
        out_specs=anywhere,
        scratch_shapes=[
            pltpu.VMEM((SPANS, PARTS, 2, PEERS, RUN, HEAD_WIDTH), jnp.bfloat16),
            pltpu.VMEM((PEERS, RUN, WIDE), jnp.bfloat16),
            pltpu.VMEM((ROWS, HEAD_WIDTH), jnp.bfloat16),
            pltpu.VMEM((PEERS, RUN, WIDE), jnp.bfloat16),
            pltpu.VMEM((level_gate.shape[0], WIDE), jnp.float32),
            pltpu.VMEM(key_value_pages.shape[1:], jnp.bfloat16),
            pltpu.VMEM((KEY_VALUE_HEADS, 2, RUN, HEAD_WIDTH), jnp.bfloat16),
            pltpu.VMEM(block_table.shape, jnp.int32),
            pltpu.VMEM(page_mask.shape, jnp.int32),
            pltpu.SMEM(noise_level.shape, jnp.int32),
            pltpu.VMEM((SPANS // 2, PARTS, 8, 128), jnp.float32),
            pltpu.VMEM((ROWS, 1), jnp.float32),
            pltpu.VMEM((ROWS, 1), jnp.float32),
            pltpu.VMEM((ROWS, HEAD_WIDTH), jnp.float32),
            dma((5,)),
            dma((3 * PEERS,)),
            dma((PARTS,)),
            dma((5,)),
            dma((PEERS,)),
            dma,
            dma((32,)),
            dma((SPANS, PARTS)),
            dma((32,)),
            dma((SPANS, PARTS)),
            dma((PEERS,)),
            dma,
        ],
        compiler_params=pltpu.CompilerParams(
            collective_id=0, has_side_effects=True, vmem_limit_bytes=16 * 1024 * 1024
        ),
    )(*(pltpu.with_memory_space_constraint(array, pltpu.HBM) for array in arrays))


def solution(mesh):
    in_specs = (P("section", "seq", None), P("section", "seq", None, None), P(), P(), P(), P())
    out_specs = P("section", "seq", None)
    return jax.shard_map(body, mesh=mesh, in_specs=in_specs, out_specs=out_specs, check_vma=False)
```

```python
import functools

import jax
import jax.numpy as jnp
from jax import lax
from jax.experimental import pallas as pl
from jax.experimental.pallas import tpu as pltpu
from jax.sharding import PartitionSpec as P

QUERY_HEADS = 32
KEY_VALUE_HEADS = 8
HEAD_WIDTH = 128
SPANS = 16
PAGES = 64
PARTS = 4
PEERS = 8
RUN = 8
GROUP = QUERY_HEADS // KEY_VALUE_HEADS
WIDE = GROUP * HEAD_WIDTH
ROWS = GROUP * PEERS * RUN
SPAN = PARTS * PEERS * RUN
EXPONENT = HEAD_WIDTH ** (-0.5) * 1.4426950408889634
HIDDEN = -3e30
MESH = pl.DeviceIdType.MESH

eps = 1e-06


def kernel(
    queries,
    pool,
    table_any,
    mask_any,
    noise_any,
    gates,
    out,
    kv,
    arrived,
    rows,
    ready,
    gate,
    raw,
    source,
    table,
    mask,
    noise,
    bias,
    top,
    total,
    accum,
    local_sem,
    spread_send,
    spread_recv,
    deep_send,
    query_send,
    query_recv,
    relay_send,
    relay_recv,
    share_send,
    share_recv,
    out_send,
    out_recv,
):
    s = lax.axis_index("section")
    t = lax.axis_index("seq")
    chip, core = s // 2, s % 2
    x, y = chip // 4, chip % 4
    column, z = t // 16, t % 16
    part = z // 4
    me = column * 4 + z % 4
    ahead, behind = column * 16 + (z + 4) % 16, column * 16 + (z + 12) % 16

    def seat(peer, block):
        return (peer // 4) * 16 + block * 4 + peer % 4

    def section(xx, yy):
        return (xx * 4 + yy) * 2 + core

    up, down = (y + 1) % 4, (y + 3) % 4
    partner = chip * 2 + 1 - core

    barrier = pltpu.get_barrier_semaphore()
    corner = section(1 - x, (y + 1 + 2 * x) % 4)
    for other in (section(x, up), section(x, down), section(1 - x, y), corner, partner):
        pl.semaphore_signal(barrier, inc=1, device_id=(other, t), device_id_type=MESH)
    for step in range(1, PEERS):
        pl.semaphore_signal(
            barrier, inc=1, device_id=(s, seat((me + step) % PEERS, part)), device_id_type=MESH
        )
    @pl.when(part == 0)
    def _():
        for block in range(1, PARTS):
            for peer in range(PEERS):
                pl.semaphore_signal(
                    barrier, inc=1, device_id=(s, seat(peer, block)), device_id_type=MESH
                )

    beside = jnp.where(part == 3, behind, ahead)

    @pl.when(part > 0)
    def _():
        pl.semaphore_signal(barrier, inc=1, device_id=(s, beside), device_id_type=MESH)

    mine = pl.ds(pl.multiple_of(me * WIDE, WIDE), WIDE)
    loads = [
        pltpu.make_async_copy(pool.at[0], raw, local_sem.at[0]),
        pltpu.make_async_copy(table_any, table, local_sem.at[1]),
        pltpu.make_async_copy(mask_any, mask, local_sem.at[2]),
        pltpu.make_async_copy(gates.at[:, mine], gate, local_sem.at[3]),
        pltpu.make_async_copy(noise_any, noise, local_sem.at[4]),
    ]
    for load in loads:
        load.start()

    loads[0].wait()
    for head in range(KEY_VALUE_HEADS):
        for kind in range(2):
            first = (kind * KEY_VALUE_HEADS + head) * HEAD_WIDTH
            for page in range(2):
                source[head, kind, page * 4 : (page + 1) * 4, :] = raw[
                    page, :, first : first + HEAD_WIDTH
                ]

    @pl.when(core == 0)
    def _():
        kv[s + 1] = jnp.zeros(kv.shape[1:], kv.dtype)

    top[...] = jnp.full(top.shape, -1e30, jnp.float32)
    total[...] = jnp.zeros(total.shape, jnp.float32)
    accum[...] = jnp.zeros(accum.shape, jnp.float32)

    expected = 12 + jnp.where(part == 0, 0, PEERS)
    expected += jnp.where(part == 2, 2, 0) + jnp.where(part == 3, 1, 0)
    pl.semaphore_wait(barrier, expected)

    sends = []

    def spread(turn, step, block, condition):
        peer = (me + step) % PEERS
        copy = pltpu.make_async_remote_copy(
            src_ref=source.at[peer],
            dst_ref=kv.at[s, part, :, me],
            send_sem=spread_send.at[turn * PEERS + step],
            recv_sem=spread_recv.at[part],
            device_id=(s, seat(peer, block)),
            device_id_type=MESH,
        )
        pl.when(condition)(copy.start)
        sends.append((condition, copy))

    for step in range(PEERS):
        spread(1, step, 0, part > 0)
    pltpu.make_async_copy(source.at[me], kv.at[s, part, :, me], spread_recv.at[part]).start()
    for step in range(1, PEERS):
        spread(0, step, part, s >= 0)
    for step in range(PEERS):
        peer = (me + step) % PEERS
        piece = queries.at[0, :, pl.ds(pl.multiple_of(peer * WIDE, WIDE), WIDE)]
        if step == 0:
            pltpu.make_async_copy(piece, arrived.at[me], query_recv).start()
            continue
        copy = pltpu.make_async_remote_copy(
            src_ref=piece,
            dst_ref=arrived.at[me],
            send_sem=query_send.at[step],
            recv_sem=query_recv,
            device_id=(s, seat(peer, part)),
            device_id_type=MESH,
        )
        copy.start()
        sends.append((None, copy))

    loads[1].wait()
    loads[2].wait()
    place = lax.broadcasted_iota(jnp.int32, (SPAN, PAGES), 0)
    holder = ((place // 32) % 2) * 16 + (place // 64) * 4 + (place // 8) % 4
    page = holder * 2 + (place % 8) // 4
    wanted = mask[pl.ds(s, 1), :].astype(jnp.float32)
    for c in range(SPANS):
        onehot = (table[c : c + 1, :] == page).astype(jnp.float32)
        row = jnp.broadcast_to(wanted[:, c * PAGES : (c + 1) * PAGES], (8, PAGES))
        seen = lax.dot_general(row, onehot, (((1,), (1,)), ((), ())))
        hide = jnp.where(seen > 0.5, 0.0, HIDDEN)
        lanes = slice((c % 2) * 64, (c % 2) * 64 + 64)
        for piece in range(PARTS):
            bias[c // 2, piece, :, lanes] = hide[:, piece * 64 : (piece + 1) * 64]

    count = [0, 0]

    def relay(slot, piece, other, condition):
        copy = pltpu.make_async_remote_copy(
            src_ref=kv.at[slot, piece],
            dst_ref=kv.at[slot, piece],
            send_sem=relay_send.at[count[0]],
            recv_sem=relay_recv.at[slot, piece],
            device_id=(other, t),
            device_id_type=MESH,
        )
        count[0] += 1
        pl.when(condition)(copy.start)
        sends.append((condition, copy))

    def share(slot, piece, condition):
        copy = pltpu.make_async_remote_copy(
            src_ref=kv.at[slot, piece],
            dst_ref=kv.at[slot, piece],
            send_sem=share_send.at[count[1]],
            recv_sem=share_recv.at[slot, piece],
            device_id=(partner, t),
            device_id_type=MESH,
        )
        count[1] += 1
        pl.when(condition)(copy.start)
        sends.append((condition, copy))

    def arrival(ref, sem):
        pltpu.make_async_copy(ref, ref, sem).wait()

    def landed(slot, piece, condition):
        @pl.when(condition)
        def _():
            arrival(kv.at[slot, piece], relay_recv.at[slot, piece])

    def attend(chunks, pieces, condition):
        @pl.when(condition)
        def _():
            scores, values = [], []
            for which in chunks:
                units = [(which * 2 + n, piece) for piece in pieces for n in range(2)]
                keys, value = (
                    jnp.concatenate(
                        [kv[a, b, kind].reshape(PEERS * RUN, HEAD_WIDTH) for a, b in units], axis=0
                    )
                    for kind in range(2)
                )
                hide = jnp.concatenate([bias[which, piece, 0:1, :] for piece in pieces], axis=1)
                score = lax.dot_general(
                    rows[...], keys, (((1,), (1,)), ((), ())), preferred_element_type=jnp.float32
                )
                scores.append(score + hide)
                values.append(value)
            before = top[...]
            peak = functools.reduce(jnp.maximum, scores)
            after = jnp.maximum(before, jnp.max(peak, axis=1, keepdims=True))
            shrink = jnp.exp2((before - after) * EXPONENT)
            weights = [jnp.exp2((score - after) * EXPONENT) for score in scores]
            top[...] = after
            mass = jnp.sum(functools.reduce(jnp.add, weights), axis=1, keepdims=True)
            total[...] = total[...] * shrink + mass
            update = accum[...] * shrink
            for weight, value in zip(weights, values):
                update += jnp.dot(
                    weight.astype(jnp.bfloat16), value, preferred_element_type=jnp.float32
                )
            accum[...] = update

    always = s >= 0
    far = x == 1

    others = [
        part,
        jnp.where(part == 3, 2, part + 1),
        jnp.where(part == 0, 2, 0),
        jnp.where(part < 2, 3, 1),
    ]

    def deep(number, piece, other, condition):
        copy = pltpu.make_async_remote_copy(
            src_ref=kv.at[s, piece],
            dst_ref=kv.at[s, piece],
            send_sem=deep_send.at[number],
            recv_sem=spread_recv.at[piece],
            device_id=(s, other),
            device_id_type=MESH,
        )
        pl.when(condition)(copy.start)
        sends.append((condition, copy))

    def collect(turn):
        piece = others[turn]
        arrival(kv.at[s, piece], spread_recv.at[piece])
        outward(piece)
        if turn == 0:
            deep(0, part, beside, part >= 2)
            deep(1, part, behind, part == 2)
        if turn == 1:
            deep(2, part, ahead, part < 2)
            deep(3, piece, behind, part == 2)
        if turn == 2:
            deep(4, piece, ahead, part == 1)
        if turn == 3:
            deep(5, part, behind, part == 0)
            deep(6, others[1], behind, part == 0)

    def outward(piece):
        relay(s, piece, section(x, up), (x == 0) | (y < 3))
        relay(s, piece, section(1, y), x == 0)
        relay(s, piece, section(x, down), y == 0)
        share(s, piece, core == 0)

    chip0, chip1, chip2 = x * 4 + down, x * 4, x * 4 + (y + 2) % 4
    chip3, chip4, chip5, chip6 = y, down, up, (y + 2) % 4
    gets0, uses0, uses1, uses2 = (x == 0) | (y >= 1), y >= 1, y == 3, y >= 2

    def early(piece):
        slot = chip0 * 2 + core
        landed(slot, piece, gets0)
        relay(slot, piece, section(1, y), x == 0)
        relay(slot, piece, section(x, up), (y == 1) | (y == 2))
        relay(slot, piece, section(1, up), x == 0)
        share(slot, piece, uses0)
        slot = chip3 * 2 + core
        landed(slot, piece, far)
        relay(slot, piece, section(1, down), far)
        share(slot, piece, far)

    def late(piece, which, condition):
        slot = which * 2 + core
        landed(slot, piece, condition)
        share(slot, piece, condition)

    def tail(piece):
        late(piece, chip4, far)
        late(piece, chip1, uses1)
        late(piece, chip2, uses2)
        late(piece, chip5, far)
        late(piece, chip6, far)

    def met(which, pieces, condition):
        slot = which * 2 + 1 - core
        for piece in pieces:

            @pl.when(condition)
            def _():
                arrival(kv.at[slot, piece], share_recv.at[slot, piece])

    def own(pieces):
        met(chip, pieces, core == 1)

    collect(0)
    arrival(arrived, query_recv)
    for head in range(GROUP):
        lanes = slice(head * HEAD_WIDTH, (head + 1) * HEAD_WIDTH)
        tall = arrived[:, :, lanes].astype(jnp.float32).reshape(PEERS * RUN, HEAD_WIDTH)
        rows[head * PEERS * RUN : (head + 1) * PEERS * RUN, :] = tall.astype(jnp.bfloat16)

    part0, part1, part2, part3 = others
    half, rest = (part0, part1), (part2, part3)
    early(part0)
    collect(1)
    tail(part0)
    early(part1)
    collect(2)
    tail(part1)
    collect(3)
    own(half)
    for which in (chip3, chip4, chip5, chip6):
        met(which, half, far)
    attend([chip], half, x == 0)
    attend([chip, chip3, chip4, chip5, chip6], half, far)
    early(part2)
    early(part3)
    met(chip0, half, uses0)
    met(chip1, half, uses1)
    met(chip2, half, uses2)
    attend([chip0], half, y == 1)
    attend([chip0, chip2], half, y == 2)
    attend([chip0, chip1, chip2], half, y == 3)
    own(rest)
    met(chip0, rest, uses0)
    met(chip3, rest, far)
    attend([chip], rest, (x == 0) & (y == 0))
    attend([chip, chip0], rest, (x == 0) & (y > 0))
    attend([chip, chip3], rest, far & (y == 0))
    attend([chip, chip0, chip3], rest, far & (y > 0))
    tail(part2)
    tail(part3)
    met(chip1, rest, uses1)
    met(chip2, rest, uses2)
    for which in (chip4, chip5, chip6):
        met(which, rest, far)
    attend([chip2], rest, (x == 0) & (y == 2))
    attend([chip1, chip2], rest, (x == 0) & (y == 3))
    attend([chip4, chip5, chip6], rest, far & (y < 2))
    attend([chip4, chip5, chip6, chip2], rest, far & (y == 2))
    attend([chip4, chip5, chip6, chip1, chip2], rest, far & (y == 3))

    loads[3].wait()
    loads[4].wait()
    level = noise[s]
    row = gate[pl.ds(level, 1), :]
    mixed = accum[...] / total[...]
    normed = mixed * lax.rsqrt(jnp.mean(mixed * mixed, axis=1, keepdims=True) + eps)
    for head in range(GROUP):
        lanes = slice(head * HEAD_WIDTH, (head + 1) * HEAD_WIDTH)
        block = normed[head * PEERS * RUN : (head + 1) * PEERS * RUN, :] * row[:, lanes]
        ready[:, :, lanes] = block.reshape(PEERS, RUN, HEAD_WIDTH).astype(jnp.bfloat16)
    pltpu.make_async_copy(ready.at[me], out.at[0, :, mine], out_recv).start()
    for step in range(1, PEERS):
        peer = (me + step) % PEERS
        copy = pltpu.make_async_remote_copy(
            src_ref=ready.at[peer],
            dst_ref=out.at[0, :, mine],
            send_sem=out_send.at[step],
            recv_sem=out_recv,
            device_id=(s, seat(peer, part)),
            device_id_type=MESH,
        )
        copy.start()
        sends.append((None, copy))

    for condition, copy in sends:
        if condition is None:
            copy.wait_send()
        else:
            pl.when(condition)(copy.wait_send)
    arrival(out, out_recv)


def body(*arrays):
    queries, key_value_pages, block_table, page_mask, noise_level, level_gate = arrays
    anywhere = pl.BlockSpec(memory_space=pl.ANY)
    dma = pltpu.SemaphoreType.DMA
    return pl.pallas_call(
        kernel,
        out_shape=jax.ShapeDtypeStruct(queries.shape, jnp.bfloat16),
        in_specs=[anywhere] * len(arrays),
        out_specs=anywhere,
        scratch_shapes=[
            pltpu.VMEM((SPANS, PARTS, 2, PEERS, RUN, HEAD_WIDTH), jnp.bfloat16),
            pltpu.VMEM((PEERS, RUN, WIDE), jnp.bfloat16),
            pltpu.VMEM((ROWS, HEAD_WIDTH), jnp.bfloat16),
            pltpu.VMEM((PEERS, RUN, WIDE), jnp.bfloat16),
            pltpu.VMEM((level_gate.shape[0], WIDE), jnp.float32),
            pltpu.VMEM(key_value_pages.shape[1:], jnp.bfloat16),
            pltpu.VMEM((KEY_VALUE_HEADS, 2, RUN, HEAD_WIDTH), jnp.bfloat16),
            pltpu.VMEM(block_table.shape, jnp.int32),
            pltpu.VMEM(page_mask.shape, jnp.int32),
            pltpu.SMEM(noise_level.shape, jnp.int32),
            pltpu.VMEM((SPANS // 2, PARTS, 8, 128), jnp.float32),
            pltpu.VMEM((ROWS, 1), jnp.float32),
            pltpu.VMEM((ROWS, 1), jnp.float32),
            pltpu.VMEM((ROWS, HEAD_WIDTH), jnp.float32),
            dma((5,)),
            dma((2 * PEERS,)),
            dma((PARTS,)),
            dma((7,)),
            dma((PEERS,)),
            dma,
            dma((32,)),
            dma((SPANS, PARTS)),
            dma((32,)),
            dma((SPANS, PARTS)),
            dma((PEERS,)),
            dma,
        ],
        compiler_params=pltpu.CompilerParams(
            collective_id=0, has_side_effects=True, vmem_limit_bytes=16 * 1024 * 1024
        ),
    )(*(pltpu.with_memory_space_constraint(array, pltpu.HBM) for array in arrays))


def solution(mesh):
    in_specs = (P("section", "seq", None), P("section", "seq", None, None), P(), P(), P(), P())
    out_specs = P("section", "seq", None)
    return jax.shard_map(body, mesh=mesh, in_specs=in_specs, out_specs=out_specs, check_vma=False)
```

```python
import functools

import jax
import jax.numpy as jnp
from jax import lax
from jax.experimental import pallas as pl
from jax.experimental.pallas import tpu as pltpu
from jax.sharding import PartitionSpec as P

QUERY_HEADS = 32
KEY_VALUE_HEADS = 8
HEAD_WIDTH = 128
SPANS = 16
PAGES = 64
PARTS = 4
PEERS = 8
RUN = 8
GROUP = QUERY_HEADS // KEY_VALUE_HEADS
WIDE = GROUP * HEAD_WIDTH
ROWS = GROUP * PEERS * RUN
SPAN = PARTS * PEERS * RUN
EXPONENT = HEAD_WIDTH ** (-0.5) * 1.4426950408889634
HIDDEN = -3e30
MESH = pl.DeviceIdType.MESH

eps = 1e-06


def kernel(
    queries,
    pool,
    table_any,
    mask_any,
    noise_any,
    gates,
    out,
    kv,
    arrived,
    rows,
    ready,
    gate,
    raw,
    source,
    table,
    mask,
    noise,
    bias,
    top,
    total,
    accum,
    local_sem,
    ready_sem,
    spread_send,
    spread_recv,
    deep_send,
    query_send,
    query_recv,
    relay_send,
    relay_recv,
    share_send,
    share_recv,
    out_send,
    out_recv,
):
    s = lax.axis_index("section")
    t = lax.axis_index("seq")
    chip, core = s // 2, s % 2
    x, y = chip // 4, chip % 4
    column, z = t // 16, t % 16
    part = z // 4
    me = column * 4 + z % 4
    ahead, behind = column * 16 + (z + 4) % 16, column * 16 + (z + 12) % 16

    def fellow(step):
        turn = (0, 2, 1, 3, 2, 1, 3, 0)[step]
        side = (me // 4 + (0 if step in (0, 4, 5, 6) else 1)) % 2
        return side * 4 + (me + turn) % 4

    def seat(peer, block):
        return (peer // 4) * 16 + block * 4 + peer % 4

    def section(xx, yy):
        return (xx * 4 + yy) * 2 + core

    up, down = (y + 1) % 4, (y + 3) % 4
    partner = chip * 2 + 1 - core

    barrier = pltpu.get_barrier_semaphore()
    corner = section(1 - x, (y + 1 + 2 * x) % 4)
    flip = 1 - 2 * core
    cross = [other + flip for other in (section(x, up), section(x, down), corner)]
    for other in (section(x, up), section(x, down), section(1 - x, y), corner, partner, *cross):
        pl.semaphore_signal(barrier, inc=1, device_id=(other, t), device_id_type=MESH)
    for step in range(1, PEERS):
        pl.semaphore_signal(
            barrier, inc=1, device_id=(s, seat(fellow(step), part)), device_id_type=MESH
        )
    @pl.when(part == 0)
    def _():
        for block in range(1, PARTS):
            for peer in range(PEERS):
                pl.semaphore_signal(
                    barrier, inc=1, device_id=(s, seat(peer, block)), device_id_type=MESH
                )

    beside = jnp.where(part % 3 == 0, behind, ahead)

    @pl.when(part > 0)
    def _():
        pl.semaphore_signal(barrier, inc=1, device_id=(s, beside), device_id_type=MESH)

    mine = pl.ds(pl.multiple_of(me * WIDE, WIDE), WIDE)
    loads = [
        pltpu.make_async_copy(pool.at[0], raw, local_sem.at[0]),
        pltpu.make_async_copy(table_any, table, local_sem.at[1]),
        pltpu.make_async_copy(mask_any, mask, local_sem.at[2]),
        pltpu.make_async_copy(gates.at[:, mine], gate, local_sem.at[3]),
        pltpu.make_async_copy(noise_any, noise, local_sem.at[4]),
    ]
    for load in loads:
        load.start()

    loads[0].wait()
    for head in range(KEY_VALUE_HEADS):
        for kind in range(2):
            first = (kind * KEY_VALUE_HEADS + head) * HEAD_WIDTH
            for page in range(2):
                source[head, kind, page * 4 : (page + 1) * 4, :] = raw[
                    page, :, first : first + HEAD_WIDTH
                ]

    @pl.when(core == 0)
    def _():
        kv[s + 1] = jnp.zeros(kv.shape[1:], kv.dtype)

    top[...] = jnp.full(top.shape, -1e30, jnp.float32)
    total[...] = jnp.zeros(total.shape, jnp.float32)
    accum[...] = jnp.zeros(accum.shape, jnp.float32)

    inner = (part == 1) | (part == 2)
    extra = jnp.where(part == 2, 2, 0) + jnp.where(part == 3, 1, 0)
    pl.semaphore_wait(barrier, 15 + jnp.where(part > 0, PEERS, 0) + extra)

    @pl.when(inner)
    def _():
        pl.semaphore_signal(ready_sem.at[0], inc=1, device_id=(s, behind), device_id_type=MESH)

    @pl.when(part == 3)
    def _():
        pl.semaphore_signal(ready_sem.at[1], inc=1, device_id=(s, ahead), device_id_type=MESH)

    sends = []

    def spread(turn, step, block, condition, kind=None):
        peer = fellow(step)
        whole = kind is None
        copy = pltpu.make_async_remote_copy(
            src_ref=source.at[peer] if whole else source.at[peer, kind],
            dst_ref=kv.at[s, part, :, me] if whole else kv.at[s, part, kind, me],
            send_sem=spread_send.at[turn * PEERS + step],
            recv_sem=spread_recv.at[part],
            device_id=(s, seat(peer, block)),
            device_id_type=MESH,
        )
        pl.when(condition)(copy.start)
        sends.append((condition, copy))

    for step in range(PEERS):
        spread(1, step, 0, inner)
        spread(1, step, 0, part == 3, 0)
    pltpu.make_async_copy(source.at[me], kv.at[s, part, :, me], spread_recv.at[part]).start()
    for step in range(1, PEERS):
        spread(0, step, part, s >= 0)
    loads[1].wait()
    loads[2].wait()
    place = lax.broadcasted_iota(jnp.int32, (SPAN, PAGES), 0)
    holder = ((place // 32) % 2) * 16 + (place // 64) * 4 + (place // 8) % 4
    page = holder * 2 + (place % 8) // 4
    wanted = mask[pl.ds(s, 1), :].astype(jnp.float32)
    for c in range(SPANS):
        onehot = (table[c : c + 1, :] == page).astype(jnp.float32)
        row = jnp.broadcast_to(wanted[:, c * PAGES : (c + 1) * PAGES], (8, PAGES))
        seen = lax.dot_general(row, onehot, (((1,), (1,)), ((), ())))
        hide = jnp.where(seen > 0.5, 0.0, HIDDEN)
        lanes = slice((c % 2) * 64, (c % 2) * 64 + 64)
        for piece in range(PARTS):
            bias[c // 2, piece, :, lanes] = hide[:, piece * 64 : (piece + 1) * 64]

    count = [0, 0]

    def relay(slot, piece, other, condition, arrivals=None):
        arrivals = relay_recv if arrivals is None else arrivals
        copy = pltpu.make_async_remote_copy(
            src_ref=kv.at[slot, piece],
            dst_ref=kv.at[slot, piece],
            send_sem=relay_send.at[count[0]],
            recv_sem=arrivals.at[slot, piece],
            device_id=(other, t),
            device_id_type=MESH,
        )
        count[0] += 1
        pl.when(condition)(copy.start)
        sends.append((condition, copy))

    def share(slot, piece, condition):
        copy = pltpu.make_async_remote_copy(
            src_ref=kv.at[slot, piece],
            dst_ref=kv.at[slot, piece],
            send_sem=share_send.at[count[1]],
            recv_sem=share_recv.at[slot, piece],
            device_id=(partner, t),
            device_id_type=MESH,
        )
        count[1] += 1
        pl.when(condition)(copy.start)
        sends.append((condition, copy))

    def arrival(ref, sem):
        pltpu.make_async_copy(ref, ref, sem).wait()

    def landed(slot, piece, condition):
        @pl.when(condition)
        def _():
            arrival(kv.at[slot, piece], relay_recv.at[slot, piece])

    def attend(chunks, pieces, condition):
        @pl.when(condition)
        def _():
            scores, values = [], []
            for which in chunks:
                units = [(which * 2 + n, piece) for piece in pieces for n in range(2)]
                keys, value = (
                    jnp.concatenate(
                        [kv[a, b, kind].reshape(PEERS * RUN, HEAD_WIDTH) for a, b in units], axis=0
                    )
                    for kind in range(2)
                )
                hide = jnp.concatenate([bias[which, piece, 0:1, :] for piece in pieces], axis=1)
                score = lax.dot_general(
                    rows[...], keys, (((1,), (1,)), ((), ())), preferred_element_type=jnp.float32
                )
                scores.append(score + hide)
                values.append(value)
            before = top[...]
            peak = functools.reduce(jnp.maximum, scores)
            after = jnp.maximum(before, jnp.max(peak, axis=1, keepdims=True))
            shrink = jnp.exp2((before - after) * EXPONENT)
            weights = [jnp.exp2((score - after) * EXPONENT) for score in scores]
            top[...] = after
            mass = jnp.sum(functools.reduce(jnp.add, weights), axis=1, keepdims=True)
            total[...] = total[...] * shrink + mass
            update = accum[...] * shrink
            for weight, value in zip(weights, values):
                update += jnp.dot(
                    weight.astype(jnp.bfloat16), value, preferred_element_type=jnp.float32
                )
            accum[...] = update

    always = s >= 0
    far = x == 1

    others = [
        part,
        1 - part % 2,
        jnp.where(part == 2, 3, 2),
        jnp.where(part < 2, 3, part - 2),
    ]

    def deep(number, piece, other, condition, kind=None):
        ref = kv.at[s, piece] if kind is None else kv.at[s, piece, kind]
        copy = pltpu.make_async_remote_copy(
            src_ref=ref,
            dst_ref=ref,
            send_sem=deep_send.at[number],
            recv_sem=spread_recv.at[piece],
            device_id=(s, other),
            device_id_type=MESH,
        )
        pl.when(condition)(copy.start)
        sends.append((condition, copy))

    def collect(turn):
        piece = others[turn]
        arrival(kv.at[s, piece], spread_recv.at[piece])
        outward(piece)
        if turn == 0:
            deep(0, part, ahead, part == 2)
            deep(0, part, ahead, part == 3, 1)
            deep(1, part, behind, part >= 2)
        if turn == 1:
            deep(4, piece, beside, part < 2)
        if turn == 2:
            deep(5, piece, behind, part == 2, 0)
        if turn == 3:
            deep(6, piece, ahead, part == 0, 1)

    def twice(slot, piece, other, condition, double):
        relay(slot, piece, other, condition)
        if double:
            relay(slot, piece, other + flip, condition, share_recv)

    def outward(piece):
        relay(s, piece, section(x, up), (x == 0) | (y < 3))
        relay(s, piece, section(1, y), x == 0)
        relay(s, piece, section(x, down), y == 0)
        relay(s, piece, section(1, up), x == 0)
        share(s, piece, core == 0)

    chip0, chip1, chip2 = x * 4 + down, x * 4, x * 4 + (y + 2) % 4
    chip3, chip4, chip5, chip6 = y, down, up, (y + 2) % 4
    gets0, uses0, uses1, uses2 = (x == 0) | (y >= 1), y >= 1, y == 3, y >= 2

    def early(piece, double=False):
        slot = chip0 * 2 + core
        landed(slot, piece, gets0)
        twice(slot, piece, section(x, up), (y == 1) | (y == 2), double)
        twice(slot, piece, section(1, up), x == 0, double)
        share(slot, piece, uses0)
        slot = chip3 * 2 + core
        landed(slot, piece, far)
        twice(slot, piece, section(1, down), far, double)
        share(slot, piece, far)

    def late(piece, which, condition, passed=True):
        slot = which * 2 + core
        landed(slot, piece, condition)
        if passed:
            share(slot, piece, condition)

    def tail(piece, passed=True):
        late(piece, chip4, far)
        late(piece, chip1, uses1)
        late(piece, chip2, uses2, passed)
        late(piece, chip5, far, passed)
        late(piece, chip6, far, passed)

    def met(which, pieces, condition):
        slot = which * 2 + 1 - core
        for piece in pieces:

            @pl.when(condition)
            def _():
                arrival(kv.at[slot, piece], share_recv.at[slot, piece])

    def own(pieces):
        met(chip, pieces, core == 1)

    collect(0)
    for step in range(PEERS):
        peer = fellow(step)
        piece = queries.at[0, :, pl.ds(pl.multiple_of(peer * WIDE, WIDE), WIDE)]
        if step == 0:
            pltpu.make_async_copy(piece, arrived.at[me], query_recv).start()
            continue
        copy = pltpu.make_async_remote_copy(
            src_ref=piece,
            dst_ref=arrived.at[me],
            send_sem=query_send.at[step],
            recv_sem=query_recv,
            device_id=(s, seat(peer, part)),
            device_id_type=MESH,
        )
        copy.start()
        sends.append((None, copy))

    part0, part1, part2, part3 = others
    half, rest = (part0, part1), (part2, part3)
    @pl.when(part < 2)
    def _():
        pl.semaphore_wait(ready_sem.at[0], 1)

    deep(2, part, ahead, part < 2)
    early(part0)

    @pl.when(part == 0)
    def _():
        pl.semaphore_wait(ready_sem.at[1], 1)

    deep(3, part, behind, part == 0)
    collect(1)
    tail(part0)
    early(part1)
    collect(2)
    arrival(arrived, query_recv)
    for head in range(GROUP):
        lanes = slice(head * HEAD_WIDTH, (head + 1) * HEAD_WIDTH)
        tall = arrived[:, :, lanes].astype(jnp.float32).reshape(PEERS * RUN, HEAD_WIDTH)
        rows[head * PEERS * RUN : (head + 1) * PEERS * RUN, :] = tall.astype(jnp.bfloat16)

    tail(part1)
    early(part2)

    def begin():
        own(half)
        for which in (chip3, chip4, chip5, chip6):
            met(which, half, far)
        attend([chip], half, x == 0)
        attend([chip, chip3, chip4, chip5, chip6], half, far)
        met(chip0, half, uses0)
        met(chip1, half, uses1)
        met(chip2, half, uses2)
        attend([chip0], half, y == 1)
        attend([chip0, chip2], half, y == 2)
        attend([chip0, chip1, chip2], half, y == 3)

    pl.when(part == 1)(begin)
    collect(3)
    pl.when(part != 1)(begin)
    early(part3, True)
    tail(part2)
    own(rest)
    met(chip0, rest, uses0)
    met(chip3, rest, far)
    attend([chip], rest, (x == 0) & (y == 0))
    attend([chip, chip0], rest, (x == 0) & (y > 0))
    attend([chip, chip3], rest, far & (y == 0))
    attend([chip, chip0, chip3], rest, far & (y > 0))
    tail(part3, False)
    met(chip1, rest, uses1)
    met(chip2, rest, uses2)
    for which in (chip4, chip5, chip6):
        met(which, rest, far)
    attend([chip2], rest, (x == 0) & (y == 2))
    attend([chip1, chip2], rest, (x == 0) & (y == 3))
    attend([chip4, chip5, chip6], rest, far & (y < 2))
    attend([chip4, chip5, chip6, chip2], rest, far & (y == 2))
    attend([chip4, chip5, chip6, chip1, chip2], rest, far & (y == 3))

    loads[3].wait()
    loads[4].wait()
    level = noise[s]
    row = gate[pl.ds(level, 1), :]
    mixed = accum[...] / total[...]
    normed = mixed * lax.rsqrt(jnp.mean(mixed * mixed, axis=1, keepdims=True) + eps)
    for head in range(GROUP):
        lanes = slice(head * HEAD_WIDTH, (head + 1) * HEAD_WIDTH)
        block = normed[head * PEERS * RUN : (head + 1) * PEERS * RUN, :] * row[:, lanes]
        ready[:, :, lanes] = block.reshape(PEERS, RUN, HEAD_WIDTH).astype(jnp.bfloat16)
    pltpu.make_async_copy(ready.at[me], out.at[0, :, mine], out_recv).start()
    for step in range(1, PEERS):
        peer = fellow(step)
        copy = pltpu.make_async_remote_copy(
            src_ref=ready.at[peer],
            dst_ref=out.at[0, :, mine],
            send_sem=out_send.at[step],
            recv_sem=out_recv,
            device_id=(s, seat(peer, part)),
            device_id_type=MESH,
        )
        copy.start()
        sends.append((None, copy))

    for condition, copy in sends:
        if condition is None:
            copy.wait_send()
        else:
            pl.when(condition)(copy.wait_send)
    arrival(out, out_recv)


def body(*arrays):
    queries, key_value_pages, block_table, page_mask, noise_level, level_gate = arrays
    anywhere = pl.BlockSpec(memory_space=pl.ANY)
    dma = pltpu.SemaphoreType.DMA
    return pl.pallas_call(
        kernel,
        out_shape=jax.ShapeDtypeStruct(queries.shape, jnp.bfloat16),
        in_specs=[anywhere] * len(arrays),
        out_specs=anywhere,
        scratch_shapes=[
            pltpu.VMEM((SPANS, PARTS, 2, PEERS, RUN, HEAD_WIDTH), jnp.bfloat16),
            pltpu.VMEM((PEERS, RUN, WIDE), jnp.bfloat16),
            pltpu.VMEM((ROWS, HEAD_WIDTH), jnp.bfloat16),
            pltpu.VMEM((PEERS, RUN, WIDE), jnp.bfloat16),
            pltpu.VMEM((level_gate.shape[0], WIDE), jnp.float32),
            pltpu.VMEM(key_value_pages.shape[1:], jnp.bfloat16),
            pltpu.VMEM((KEY_VALUE_HEADS, 2, RUN, HEAD_WIDTH), jnp.bfloat16),
            pltpu.VMEM(block_table.shape, jnp.int32),
            pltpu.VMEM(page_mask.shape, jnp.int32),
            pltpu.SMEM(noise_level.shape, jnp.int32),
            pltpu.VMEM((SPANS // 2, PARTS, 8, 128), jnp.float32),
            pltpu.VMEM((ROWS, 1), jnp.float32),
            pltpu.VMEM((ROWS, 1), jnp.float32),
            pltpu.VMEM((ROWS, HEAD_WIDTH), jnp.float32),
            dma((5,)),
            pltpu.SemaphoreType.REGULAR((2,)),
            dma((2 * PEERS,)),
            dma((PARTS,)),
            dma((7,)),
            dma((PEERS,)),
            dma,
            dma((32,)),
            dma((SPANS, PARTS)),
            dma((32,)),
            dma((SPANS, PARTS)),
            dma((PEERS,)),
            dma,
        ],
        compiler_params=pltpu.CompilerParams(
            collective_id=0, has_side_effects=True, vmem_limit_bytes=16 * 1024 * 1024
        ),
    )(*(pltpu.with_memory_space_constraint(array, pltpu.HBM) for array in arrays))


def solution(mesh):
    in_specs = (P("section", "seq", None), P("section", "seq", None, None), P(), P(), P(), P())
    out_specs = P("section", "seq", None)
    return jax.shard_map(body, mesh=mesh, in_specs=in_specs, out_specs=out_specs, check_vma=False)
```

```python
import functools

import jax
import jax.numpy as jnp
from jax import lax
from jax.experimental import pallas as pl
from jax.experimental.pallas import tpu as pltpu
from jax.sharding import PartitionSpec as P

QUERY_HEADS = 32
KEY_VALUE_HEADS = 8
HEAD_WIDTH = 128
SPANS = 16
PAGES = 64
PARTS = 4
PEERS = 8
RUN = 8
GROUP = QUERY_HEADS // KEY_VALUE_HEADS
WIDE = GROUP * HEAD_WIDTH
ROWS = GROUP * PEERS * RUN
SPAN = PARTS * PEERS * RUN
EXPONENT = HEAD_WIDTH ** (-0.5) * 1.4426950408889634
HIDDEN = -3e30
MESH = pl.DeviceIdType.MESH

eps = 1e-06


def kernel(
    queries,
    pool,
    table_any,
    mask_any,
    noise_any,
    gates,
    out,
    kv,
    arrived,
    rows,
    ready,
    gate,
    raw,
    source,
    table,
    mask,
    noise,
    bias,
    top,
    total,
    accum,
    local_sem,
    ready_sem,
    spread_send,
    spread_recv,
    deep_send,
    query_send,
    query_recv,
    relay_send,
    relay_recv,
    share_send,
    share_recv,
    out_send,
    out_recv,
):
    s = lax.axis_index("section")
    t = lax.axis_index("seq")
    chip, core = s // 2, s % 2
    x, y = chip // 4, chip % 4
    column, z = t // 16, t % 16
    part = z // 4
    me = column * 4 + z % 4
    ahead, behind = column * 16 + (z + 4) % 16, column * 16 + (z + 12) % 16

    def fellow(step):
        turn = (0, 2, 1, 3, 2, 1, 3, 0)[step]
        side = (me // 4 + (0 if step in (0, 4, 5, 6) else 1)) % 2
        return side * 4 + (me + turn) % 4

    def seat(peer, block):
        return (peer // 4) * 16 + block * 4 + peer % 4

    def section(xx, yy):
        return (xx * 4 + yy) * 2 + core

    up, down = (y + 1) % 4, (y + 3) % 4
    partner = chip * 2 + 1 - core

    barrier = pltpu.get_barrier_semaphore()
    corner = section(1 - x, (y + 1 + 2 * x) % 4)
    flip = 1 - 2 * core
    cross = [other + flip for other in (section(x, up), section(x, down), corner)]
    for other in (section(x, up), section(x, down), section(1 - x, y), corner, partner, *cross):
        pl.semaphore_signal(barrier, inc=1, device_id=(other, t), device_id_type=MESH)
    for step in range(1, PEERS):
        pl.semaphore_signal(
            barrier, inc=1, device_id=(s, seat(fellow(step), part)), device_id_type=MESH
        )
    @pl.when(part == 0)
    def _():
        for block in range(1, PARTS):
            for peer in range(PEERS):
                pl.semaphore_signal(
                    barrier, inc=1, device_id=(s, seat(peer, block)), device_id_type=MESH
                )

    beside = jnp.where(part % 3 == 0, behind, ahead)

    @pl.when(part > 0)
    def _():
        pl.semaphore_signal(barrier, inc=1, device_id=(s, beside), device_id_type=MESH)

    mine = pl.ds(pl.multiple_of(me * WIDE, WIDE), WIDE)
    loads = [
        pltpu.make_async_copy(pool.at[0], raw, local_sem.at[0]),
        pltpu.make_async_copy(table_any, table, local_sem.at[1]),
        pltpu.make_async_copy(mask_any, mask, local_sem.at[2]),
        pltpu.make_async_copy(gates.at[:, mine], gate, local_sem.at[3]),
        pltpu.make_async_copy(noise_any, noise, local_sem.at[4]),
    ]
    for load in loads:
        load.start()

    loads[0].wait()
    for head in range(KEY_VALUE_HEADS):
        for kind in range(2):
            first = (kind * KEY_VALUE_HEADS + head) * HEAD_WIDTH
            for page in range(2):
                source[head, kind, page * 4 : (page + 1) * 4, :] = raw[
                    page, :, first : first + HEAD_WIDTH
                ]

    @pl.when(core == 0)
    def _():
        kv[s + 1] = jnp.zeros(kv.shape[1:], kv.dtype)

    top[...] = jnp.full(top.shape, -1e30, jnp.float32)
    total[...] = jnp.zeros(total.shape, jnp.float32)
    accum[...] = jnp.zeros(accum.shape, jnp.float32)

    inner = (part == 1) | (part == 2)
    extra = jnp.where(part == 2, 2, 0) + jnp.where(part == 3, 1, 0)
    pl.semaphore_wait(barrier, 15 + jnp.where(part > 0, PEERS, 0) + extra)

    @pl.when(inner)
    def _():
        pl.semaphore_signal(ready_sem.at[0], inc=1, device_id=(s, behind), device_id_type=MESH)

    @pl.when(part == 3)
    def _():
        pl.semaphore_signal(ready_sem.at[1], inc=1, device_id=(s, ahead), device_id_type=MESH)

    sends = []

    def spread(turn, step, block, condition, kind=None):
        peer = fellow(step)
        whole = kind is None
        copy = pltpu.make_async_remote_copy(
            src_ref=source.at[peer] if whole else source.at[peer, kind],
            dst_ref=kv.at[s, part, :, me] if whole else kv.at[s, part, kind, me],
            send_sem=spread_send.at[turn * PEERS + step],
            recv_sem=spread_recv.at[part],
            device_id=(s, seat(peer, block)),
            device_id_type=MESH,
        )
        pl.when(condition)(copy.start)
        sends.append((condition, copy))

    for step in range(PEERS):
        spread(1, step, 0, inner)
        spread(1, step, 0, part == 3, 0)
    pltpu.make_async_copy(source.at[me], kv.at[s, part, :, me], spread_recv.at[part]).start()
    for step in range(1, PEERS):
        spread(0, step, part, s >= 0)
    loads[1].wait()
    loads[2].wait()
    place = lax.broadcasted_iota(jnp.int32, (SPAN, PAGES), 0)
    holder = ((place // 32) % 2) * 16 + (place // 64) * 4 + (place // 8) % 4
    page = holder * 2 + (place % 8) // 4
    wanted = mask[pl.ds(s, 1), :].astype(jnp.float32)
    for c in range(SPANS):
        onehot = (table[c : c + 1, :] == page).astype(jnp.float32)
        row = jnp.broadcast_to(wanted[:, c * PAGES : (c + 1) * PAGES], (8, PAGES))
        seen = lax.dot_general(row, onehot, (((1,), (1,)), ((), ())))
        hide = jnp.where(seen > 0.5, 0.0, HIDDEN)
        lanes = slice((c % 2) * 64, (c % 2) * 64 + 64)
        for piece in range(PARTS):
            bias[c // 2, piece, :, lanes] = hide[:, piece * 64 : (piece + 1) * 64]

    count = [0, 0]

    def relay(slot, piece, other, condition, arrivals=None):
        arrivals = relay_recv if arrivals is None else arrivals
        copy = pltpu.make_async_remote_copy(
            src_ref=kv.at[slot, piece],
            dst_ref=kv.at[slot, piece],
            send_sem=relay_send.at[count[0]],
            recv_sem=arrivals.at[slot, piece],
            device_id=(other, t),
            device_id_type=MESH,
        )
        count[0] += 1
        pl.when(condition)(copy.start)
        sends.append((condition, copy))

    def share(slot, piece, condition):
        copy = pltpu.make_async_remote_copy(
            src_ref=kv.at[slot, piece],
            dst_ref=kv.at[slot, piece],
            send_sem=share_send.at[count[1]],
            recv_sem=share_recv.at[slot, piece],
            device_id=(partner, t),
            device_id_type=MESH,
        )
        count[1] += 1
        pl.when(condition)(copy.start)
        sends.append((condition, copy))

    def arrival(ref, sem):
        pltpu.make_async_copy(ref, ref, sem).wait()

    def landed(slot, piece, condition):
        @pl.when(condition)
        def _():
            arrival(kv.at[slot, piece], relay_recv.at[slot, piece])

    def attend(chunks, pieces, condition):
        @pl.when(condition)
        def _():
            scores, values = [], []
            for which in chunks:
                units = [(which * 2 + n, piece) for piece in pieces for n in range(2)]
                keys, value = (
                    jnp.concatenate(
                        [kv[a, b, kind].reshape(PEERS * RUN, HEAD_WIDTH) for a, b in units], axis=0
                    )
                    for kind in range(2)
                )
                hide = jnp.concatenate([bias[which, piece, 0:1, :] for piece in pieces], axis=1)
                score = lax.dot_general(
                    rows[...], keys, (((1,), (1,)), ((), ())), preferred_element_type=jnp.float32
                )
                scores.append(score + hide)
                values.append(value)
            before = top[...]
            peak = functools.reduce(jnp.maximum, scores)
            after = jnp.maximum(before, jnp.max(peak, axis=1, keepdims=True))
            shrink = jnp.exp2((before - after) * EXPONENT)
            weights = [jnp.exp2((score - after) * EXPONENT) for score in scores]
            top[...] = after
            mass = jnp.sum(functools.reduce(jnp.add, weights), axis=1, keepdims=True)
            total[...] = total[...] * shrink + mass
            update = accum[...] * shrink
            for weight, value in zip(weights, values):
                update += jnp.dot(
                    weight.astype(jnp.bfloat16), value, preferred_element_type=jnp.float32
                )
            accum[...] = update

    always = s >= 0
    far = x == 1

    others = [
        part,
        1 - part % 2,
        jnp.where(part == 2, 3, 2),
        jnp.where(part < 2, 3, part - 2),
    ]

    def deep(number, piece, other, condition, kind=None):
        ref = kv.at[s, piece] if kind is None else kv.at[s, piece, kind]
        copy = pltpu.make_async_remote_copy(
            src_ref=ref,
            dst_ref=ref,
            send_sem=deep_send.at[number],
            recv_sem=spread_recv.at[piece],
            device_id=(s, other),
            device_id_type=MESH,
        )
        pl.when(condition)(copy.start)
        sends.append((condition, copy))

    def collect(turn):
        piece = others[turn]
        arrival(kv.at[s, piece], spread_recv.at[piece])
        outward(piece)
        if turn == 0:
            deep(0, part, ahead, part == 2)
            deep(0, part, ahead, part == 3, 1)
            deep(1, part, behind, part >= 2)
        if turn == 1:
            deep(4, piece, beside, part < 2)
        if turn == 2:
            deep(5, piece, behind, part == 2, 0)
        if turn == 3:
            deep(6, piece, ahead, part == 0, 1)

    def twice(slot, piece, other, condition, double):
        relay(slot, piece, other, condition)
        if double:
            relay(slot, piece, other + flip, condition, share_recv)

    def outward(piece):
        relay(s, piece, section(x, up), (x == 0) | (y < 3))
        relay(s, piece, section(1, y), x == 0)
        relay(s, piece, section(x, down), y == 0)
        relay(s, piece, section(1, up), x == 0)
        share(s, piece, core == 0)

    chip0, chip1, chip2 = x * 4 + down, x * 4, x * 4 + (y + 2) % 4
    chip3, chip4, chip5, chip6 = y, down, up, (y + 2) % 4
    gets0, uses0, uses1, uses2 = (x == 0) | (y >= 1), y >= 1, y == 3, y >= 2

    def early(piece, double=False):
        slot = chip0 * 2 + core
        landed(slot, piece, gets0)
        twice(slot, piece, section(x, up), (y == 1) | (y == 2), double)
        twice(slot, piece, section(1, up), x == 0, double)
        share(slot, piece, uses0)
        slot = chip3 * 2 + core
        landed(slot, piece, far)
        twice(slot, piece, section(1, down), far, double)
        share(slot, piece, far)

    def late(piece, which, condition, passed=True):
        slot = which * 2 + core
        landed(slot, piece, condition)
        if passed:
            share(slot, piece, condition)

    def tail(piece, passed=True):
        late(piece, chip4, far)
        late(piece, chip1, uses1)
        late(piece, chip2, uses2, passed)
        late(piece, chip5, far, passed)
        late(piece, chip6, far, passed)

    def met(which, pieces, condition):
        slot = which * 2 + 1 - core
        for piece in pieces:

            @pl.when(condition)
            def _():
                arrival(kv.at[slot, piece], share_recv.at[slot, piece])

    def own(pieces):
        met(chip, pieces, core == 1)

    collect(0)
    for step in range(PEERS):
        peer = fellow(step)
        piece = queries.at[0, :, pl.ds(pl.multiple_of(peer * WIDE, WIDE), WIDE)]
        if step == 0:
            pltpu.make_async_copy(piece, arrived.at[me], query_recv).start()
            continue
        copy = pltpu.make_async_remote_copy(
            src_ref=piece,
            dst_ref=arrived.at[me],
            send_sem=query_send.at[step],
            recv_sem=query_recv,
            device_id=(s, seat(peer, part)),
            device_id_type=MESH,
        )
        copy.start()
        sends.append((None, copy))

    part0, part1, part2, part3 = others
    half, rest = (part0, part1), (part2, part3)
    @pl.when(part < 2)
    def _():
        pl.semaphore_wait(ready_sem.at[0], 1)

    deep(2, part, ahead, part < 2)
    early(part0)

    @pl.when(part == 0)
    def _():
        pl.semaphore_wait(ready_sem.at[1], 1)

    deep(3, part, behind, part == 0)
    collect(1)
    tail(part0)
    early(part1)
    collect(2)
    arrival(arrived, query_recv)
    for head in range(GROUP):
        lanes = slice(head * HEAD_WIDTH, (head + 1) * HEAD_WIDTH)
        tall = arrived[:, :, lanes].astype(jnp.float32).reshape(PEERS * RUN, HEAD_WIDTH)
        rows[head * PEERS * RUN : (head + 1) * PEERS * RUN, :] = tall.astype(jnp.bfloat16)

    tail(part1)
    early(part2)

    def begin():
        own(half)
        for which in (chip3, chip4, chip5, chip6):
            met(which, half, far)
        attend([chip], half, x == 0)
        attend([chip, chip3, chip4, chip5, chip6], half, far)
        met(chip0, half, uses0)
        met(chip1, half, uses1)
        met(chip2, half, uses2)
        attend([chip0], half, y == 1)
        attend([chip0, chip2], half, y == 2)
        attend([chip0, chip1, chip2], half, y == 3)

    pl.when(part == 1)(begin)
    collect(3)
    pl.when(part != 1)(begin)
    early(part3, True)
    tail(part2)
    late(part3, chip4, far)
    late(part3, chip1, uses1)

    def finish(piece):
        met(chip1, piece, uses1)
        met(chip2, piece, uses2)
        for which in (chip4, chip5, chip6):
            met(which, piece, far)
        attend([chip2], piece, (x == 0) & (y == 2))
        attend([chip1, chip2], piece, (x == 0) & (y == 3))
        attend([chip4, chip5, chip6], piece, far & (y < 2))
        attend([chip4, chip5, chip6, chip2], piece, far & (y == 2))
        attend([chip4, chip5, chip6, chip1, chip2], piece, far & (y == 3))

    finish((part2,))
    own(rest)
    met(chip0, rest, uses0)
    met(chip3, rest, far)
    attend([chip], rest, (x == 0) & (y == 0))
    attend([chip, chip0], rest, (x == 0) & (y > 0))
    attend([chip, chip3], rest, far & (y == 0))
    attend([chip, chip0, chip3], rest, far & (y > 0))
    late(part3, chip2, uses2, False)
    late(part3, chip5, far, False)
    late(part3, chip6, far, False)
    finish((part3,))

    loads[3].wait()
    loads[4].wait()
    level = noise[s]
    row = gate[pl.ds(level, 1), :]
    mixed = accum[...] / total[...]
    normed = mixed * lax.rsqrt(jnp.mean(mixed * mixed, axis=1, keepdims=True) + eps)
    for head in range(GROUP):
        lanes = slice(head * HEAD_WIDTH, (head + 1) * HEAD_WIDTH)
        block = normed[head * PEERS * RUN : (head + 1) * PEERS * RUN, :] * row[:, lanes]
        ready[:, :, lanes] = block.reshape(PEERS, RUN, HEAD_WIDTH).astype(jnp.bfloat16)
    pltpu.make_async_copy(ready.at[me], out.at[0, :, mine], out_recv).start()
    for step in range(1, PEERS):
        peer = fellow(step)
        copy = pltpu.make_async_remote_copy(
            src_ref=ready.at[peer],
            dst_ref=out.at[0, :, mine],
            send_sem=out_send.at[step],
            recv_sem=out_recv,
            device_id=(s, seat(peer, part)),
            device_id_type=MESH,
        )
        copy.start()
        sends.append((None, copy))

    for condition, copy in sends:
        if condition is None:
            copy.wait_send()
        else:
            pl.when(condition)(copy.wait_send)
    arrival(out, out_recv)


def body(*arrays):
    queries, key_value_pages, block_table, page_mask, noise_level, level_gate = arrays
    anywhere = pl.BlockSpec(memory_space=pl.ANY)
    dma = pltpu.SemaphoreType.DMA
    return pl.pallas_call(
        kernel,
        out_shape=jax.ShapeDtypeStruct(queries.shape, jnp.bfloat16),
        in_specs=[anywhere] * len(arrays),
        out_specs=anywhere,
        scratch_shapes=[
            pltpu.VMEM((SPANS, PARTS, 2, PEERS, RUN, HEAD_WIDTH), jnp.bfloat16),
            pltpu.VMEM((PEERS, RUN, WIDE), jnp.bfloat16),
            pltpu.VMEM((ROWS, HEAD_WIDTH), jnp.bfloat16),
            pltpu.VMEM((PEERS, RUN, WIDE), jnp.bfloat16),
            pltpu.VMEM((level_gate.shape[0], WIDE), jnp.float32),
            pltpu.VMEM(key_value_pages.shape[1:], jnp.bfloat16),
            pltpu.VMEM((KEY_VALUE_HEADS, 2, RUN, HEAD_WIDTH), jnp.bfloat16),
            pltpu.VMEM(block_table.shape, jnp.int32),
            pltpu.VMEM(page_mask.shape, jnp.int32),
            pltpu.SMEM(noise_level.shape, jnp.int32),
            pltpu.VMEM((SPANS // 2, PARTS, 8, 128), jnp.float32),
            pltpu.VMEM((ROWS, 1), jnp.float32),
            pltpu.VMEM((ROWS, 1), jnp.float32),
            pltpu.VMEM((ROWS, HEAD_WIDTH), jnp.float32),
            dma((5,)),
            pltpu.SemaphoreType.REGULAR((2,)),
            dma((2 * PEERS,)),
            dma((PARTS,)),
            dma((7,)),
            dma((PEERS,)),
            dma,
            dma((32,)),
            dma((SPANS, PARTS)),
            dma((32,)),
            dma((SPANS, PARTS)),
            dma((PEERS,)),
            dma,
        ],
        compiler_params=pltpu.CompilerParams(
            collective_id=0, has_side_effects=True, vmem_limit_bytes=16 * 1024 * 1024
        ),
    )(*(pltpu.with_memory_space_constraint(array, pltpu.HBM) for array in arrays))


def solution(mesh):
    in_specs = (P("section", "seq", None), P("section", "seq", None, None), P(), P(), P(), P())
    out_specs = P("section", "seq", None)
    return jax.shard_map(body, mesh=mesh, in_specs=in_specs, out_specs=out_specs, check_vma=False)
```

```python
import functools

import jax
import jax.numpy as jnp
from jax import lax
from jax.experimental import pallas as pl
from jax.experimental.pallas import tpu as pltpu
from jax.sharding import PartitionSpec as P

QUERY_HEADS = 32
KEY_VALUE_HEADS = 8
HEAD_WIDTH = 128
SPANS = 16
PAGES = 64
PARTS = 4
PEERS = 8
RUN = 8
GROUP = QUERY_HEADS // KEY_VALUE_HEADS
WIDE = GROUP * HEAD_WIDTH
ROWS = GROUP * PEERS * RUN
SPAN = PARTS * PEERS * RUN
EXPONENT = HEAD_WIDTH ** (-0.5) * 1.4426950408889634
HIDDEN = -3e30
MESH = pl.DeviceIdType.MESH

eps = 1e-06


def kernel(
    queries,
    pool,
    table_any,
    mask_any,
    noise_any,
    gates,
    out,
    kv,
    arrived,
    rows,
    ready,
    gate,
    raw,
    source,
    table,
    mask,
    noise,
    bias,
    top,
    total,
    accum,
    local_sem,
    ready_sem,
    spread_send,
    spread_recv,
    deep_send,
    query_send,
    query_recv,
    relay_send,
    relay_recv,
    share_send,
    share_recv,
    out_send,
    out_recv,
):
    s = lax.axis_index("section")
    t = lax.axis_index("seq")
    chip, core = s // 2, s % 2
    x, y = chip // 4, chip % 4
    column, z = t // 16, t % 16
    part = z // 4
    me = column * 4 + z % 4
    ahead, behind = column * 16 + (z + 4) % 16, column * 16 + (z + 12) % 16

    def fellow(step):
        turn = (0, 2, 1, 3, 2, 1, 3, 0)[step]
        side = (me // 4 + (0 if step in (0, 4, 5, 6) else 1)) % 2
        return side * 4 + (me + turn) % 4

    def seat(peer, block):
        return (peer // 4) * 16 + block * 4 + peer % 4

    def section(xx, yy):
        return (xx * 4 + yy) * 2 + core

    up, down = (y + 1) % 4, (y + 3) % 4
    partner = chip * 2 + 1 - core

    barrier = pltpu.get_barrier_semaphore()
    corner = section(1 - x, (y + 1 + 2 * x) % 4)
    flip = 1 - 2 * core
    beyond = (section(x, up), section(x, down), section(1 - x, y), corner)
    cross = [other + flip for other in beyond]
    for other in (section(x, up), section(x, down), section(1 - x, y), corner, partner, *cross):
        pl.semaphore_signal(barrier, inc=1, device_id=(other, t), device_id_type=MESH)
    for step in range(1, PEERS):
        pl.semaphore_signal(
            barrier, inc=1, device_id=(s, seat(fellow(step), part)), device_id_type=MESH
        )
    @pl.when(part == 0)
    def _():
        for block in range(1, PARTS):
            for peer in range(PEERS):
                pl.semaphore_signal(
                    barrier, inc=1, device_id=(s, seat(peer, block)), device_id_type=MESH
                )

    beside = jnp.where(part % 3 == 0, behind, ahead)

    @pl.when(part > 0)
    def _():
        pl.semaphore_signal(barrier, inc=1, device_id=(s, beside), device_id_type=MESH)

    mine = pl.ds(pl.multiple_of(me * WIDE, WIDE), WIDE)
    loads = [
        pltpu.make_async_copy(pool.at[0], raw, local_sem.at[0]),
        pltpu.make_async_copy(table_any, table, local_sem.at[1]),
        pltpu.make_async_copy(mask_any, mask, local_sem.at[2]),
        pltpu.make_async_copy(gates.at[:, mine], gate, local_sem.at[3]),
        pltpu.make_async_copy(noise_any, noise, local_sem.at[4]),
    ]
    for load in loads:
        load.start()

    loads[0].wait()
    for head in range(KEY_VALUE_HEADS):
        for kind in range(2):
            first = (kind * KEY_VALUE_HEADS + head) * HEAD_WIDTH
            for page in range(2):
                source[head, kind, page * 4 : (page + 1) * 4, :] = raw[
                    page, :, first : first + HEAD_WIDTH
                ]

    @pl.when(core == 0)
    def _():
        kv[s + 1] = jnp.zeros(kv.shape[1:], kv.dtype)

    top[...] = jnp.full(top.shape, -1e30, jnp.float32)
    total[...] = jnp.zeros(total.shape, jnp.float32)
    accum[...] = jnp.zeros(accum.shape, jnp.float32)

    inner = (part == 1) | (part == 2)
    extra = jnp.where(part == 2, 2, 0) + jnp.where(part == 3, 1, 0)
    pl.semaphore_wait(barrier, 16 + jnp.where(part > 0, PEERS, 0) + extra)

    @pl.when(inner)
    def _():
        pl.semaphore_signal(ready_sem.at[0], inc=1, device_id=(s, behind), device_id_type=MESH)

    @pl.when(part == 3)
    def _():
        pl.semaphore_signal(ready_sem.at[1], inc=1, device_id=(s, ahead), device_id_type=MESH)

    sends = []

    def spread(turn, step, block, condition, kind=None):
        peer = fellow(step)
        whole = kind is None
        copy = pltpu.make_async_remote_copy(
            src_ref=source.at[peer] if whole else source.at[peer, kind],
            dst_ref=kv.at[s, part, :, me] if whole else kv.at[s, part, kind, me],
            send_sem=spread_send.at[turn * PEERS + step],
            recv_sem=spread_recv.at[part],
            device_id=(s, seat(peer, block)),
            device_id_type=MESH,
        )
        pl.when(condition)(copy.start)
        sends.append((condition, copy))

    for step in range(PEERS):
        spread(1, step, 0, inner)
        spread(1, step, 0, part == 3, 0)
    pltpu.make_async_copy(source.at[me], kv.at[s, part, :, me], spread_recv.at[part]).start()
    for step in range(1, PEERS):
        spread(0, step, part, s >= 0)
    loads[1].wait()
    loads[2].wait()
    place = lax.broadcasted_iota(jnp.int32, (SPAN, PAGES), 0)
    holder = ((place // 32) % 2) * 16 + (place // 64) * 4 + (place // 8) % 4
    page = holder * 2 + (place % 8) // 4
    wanted = mask[pl.ds(s, 1), :].astype(jnp.float32)
    for c in range(SPANS):
        onehot = (table[c : c + 1, :] == page).astype(jnp.float32)
        row = jnp.broadcast_to(wanted[:, c * PAGES : (c + 1) * PAGES], (8, PAGES))
        seen = lax.dot_general(row, onehot, (((1,), (1,)), ((), ())))
        hide = jnp.where(seen > 0.5, 0.0, HIDDEN)
        lanes = slice((c % 2) * 64, (c % 2) * 64 + 64)
        for piece in range(PARTS):
            bias[c // 2, piece, :, lanes] = hide[:, piece * 64 : (piece + 1) * 64]

    count = [0, 0]

    def relay(slot, piece, other, condition, arrivals=None):
        arrivals = relay_recv if arrivals is None else arrivals
        copy = pltpu.make_async_remote_copy(
            src_ref=kv.at[slot, piece],
            dst_ref=kv.at[slot, piece],
            send_sem=relay_send.at[count[0]],
            recv_sem=arrivals.at[slot, piece],
            device_id=(other, t),
            device_id_type=MESH,
        )
        count[0] += 1
        pl.when(condition)(copy.start)
        sends.append((condition, copy))

    def share(slot, piece, condition):
        copy = pltpu.make_async_remote_copy(
            src_ref=kv.at[slot, piece],
            dst_ref=kv.at[slot, piece],
            send_sem=share_send.at[count[1]],
            recv_sem=share_recv.at[slot, piece],
            device_id=(partner, t),
            device_id_type=MESH,
        )
        count[1] += 1
        pl.when(condition)(copy.start)
        sends.append((condition, copy))

    def arrival(ref, sem):
        pltpu.make_async_copy(ref, ref, sem).wait()

    def landed(slot, piece, condition):
        @pl.when(condition)
        def _():
            arrival(kv.at[slot, piece], relay_recv.at[slot, piece])

    def attend(chunks, pieces, condition):
        @pl.when(condition)
        def _():
            scores, values = [], []
            for which in chunks:
                units = [(which * 2 + n, piece) for piece in pieces for n in range(2)]
                keys, value = (
                    jnp.concatenate(
                        [kv[a, b, kind].reshape(PEERS * RUN, HEAD_WIDTH) for a, b in units], axis=0
                    )
                    for kind in range(2)
                )
                hide = jnp.concatenate([bias[which, piece, 0:1, :] for piece in pieces], axis=1)
                score = lax.dot_general(
                    rows[...], keys, (((1,), (1,)), ((), ())), preferred_element_type=jnp.float32
                )
                scores.append(score + hide)
                values.append(value)
            before = top[...]
            peak = functools.reduce(jnp.maximum, scores)
            after = jnp.maximum(before, jnp.max(peak, axis=1, keepdims=True))
            shrink = jnp.exp2((before - after) * EXPONENT)
            weights = [jnp.exp2((score - after) * EXPONENT) for score in scores]
            top[...] = after
            mass = jnp.sum(functools.reduce(jnp.add, weights), axis=1, keepdims=True)
            total[...] = total[...] * shrink + mass
            update = accum[...] * shrink
            for weight, value in zip(weights, values):
                update += jnp.dot(
                    weight.astype(jnp.bfloat16), value, preferred_element_type=jnp.float32
                )
            accum[...] = update

    always = s >= 0
    far = x == 1

    others = [
        part,
        1 - part % 2,
        jnp.where(part == 2, 3, 2),
        jnp.where(part < 2, 3, part - 2),
    ]

    def deep(number, piece, other, condition, kind=None):
        ref = kv.at[s, piece] if kind is None else kv.at[s, piece, kind]
        copy = pltpu.make_async_remote_copy(
            src_ref=ref,
            dst_ref=ref,
            send_sem=deep_send.at[number],
            recv_sem=spread_recv.at[piece],
            device_id=(s, other),
            device_id_type=MESH,
        )
        pl.when(condition)(copy.start)
        sends.append((condition, copy))

    def collect(turn):
        piece = others[turn]
        arrival(kv.at[s, piece], spread_recv.at[piece])
        outward(piece, turn == 3)
        if turn == 0:
            deep(0, part, ahead, part == 2)
            deep(0, part, ahead, part == 3, 1)
            deep(1, part, behind, part >= 2)
        if turn == 1:
            deep(4, piece, beside, part < 2)
        if turn == 2:
            deep(5, piece, behind, part == 2, 0)
        if turn == 3:
            deep(6, piece, ahead, part == 0, 1)

    def twice(slot, piece, other, condition, double):
        relay(slot, piece, other, condition)
        if double:
            relay(slot, piece, other + flip, condition, share_recv)

    def outward(piece, double=False):
        relay(s, piece, section(x, up), (x == 0) | (y < 3))
        twice(s, piece, section(1, y), x == 0, double)
        twice(s, piece, section(x, down), y == 0, double)
        twice(s, piece, section(1, up), x == 0, double)
        if double:
            relay(s, piece, section(x, up) + flip, y < 3, share_recv)
        share(s, piece, core == 0)

    chip0, chip1, chip2 = x * 4 + down, x * 4, x * 4 + (y + 2) % 4
    chip3, chip4, chip5, chip6 = y, down, up, (y + 2) % 4
    gets0, uses0, uses1, uses2 = (x == 0) | (y >= 1), y >= 1, y == 3, y >= 2

    def early(piece, double=False):
        slot = chip0 * 2 + core
        landed(slot, piece, gets0)
        twice(slot, piece, section(x, up), (y == 1) | (y == 2), double)
        twice(slot, piece, section(1, up), x == 0, double)
        if not double:
            share(slot, piece, uses0)
        slot = chip3 * 2 + core
        landed(slot, piece, far)
        twice(slot, piece, section(1, down), far, double)
        if not double:
            share(slot, piece, far)

    def late(piece, which, condition, passed=True):
        slot = which * 2 + core
        landed(slot, piece, condition)
        if passed:
            share(slot, piece, condition)

    def tail(piece, passed=True):
        late(piece, chip4, far, passed)
        late(piece, chip1, uses1, passed)
        late(piece, chip2, uses2, passed)
        late(piece, chip5, far, passed)
        late(piece, chip6, far, passed)

    def met(which, pieces, condition):
        slot = which * 2 + 1 - core
        for piece in pieces:

            @pl.when(condition)
            def _():
                arrival(kv.at[slot, piece], share_recv.at[slot, piece])

    def own(pieces):
        met(chip, pieces, core == 1)

    collect(0)
    for step in range(PEERS):
        peer = fellow(step)
        piece = queries.at[0, :, pl.ds(pl.multiple_of(peer * WIDE, WIDE), WIDE)]
        if step == 0:
            pltpu.make_async_copy(piece, arrived.at[me], query_recv).start()
            continue
        copy = pltpu.make_async_remote_copy(
            src_ref=piece,
            dst_ref=arrived.at[me],
            send_sem=query_send.at[step],
            recv_sem=query_recv,
            device_id=(s, seat(peer, part)),
            device_id_type=MESH,
        )
        copy.start()
        sends.append((None, copy))

    part0, part1, part2, part3 = others
    half, rest = (part0, part1), (part2, part3)
    @pl.when(part < 2)
    def _():
        pl.semaphore_wait(ready_sem.at[0], 1)

    deep(2, part, ahead, part < 2)
    early(part0)

    @pl.when(part == 0)
    def _():
        pl.semaphore_wait(ready_sem.at[1], 1)

    deep(3, part, behind, part == 0)
    collect(1)
    tail(part0)
    early(part1)
    collect(2)
    arrival(arrived, query_recv)
    for head in range(GROUP):
        lanes = slice(head * HEAD_WIDTH, (head + 1) * HEAD_WIDTH)
        tall = arrived[:, :, lanes].astype(jnp.float32).reshape(PEERS * RUN, HEAD_WIDTH)
        rows[head * PEERS * RUN : (head + 1) * PEERS * RUN, :] = tall.astype(jnp.bfloat16)

    tail(part1)
    early(part2)

    def begin():
        own(half)
        for which in (chip3, chip4, chip5, chip6):
            met(which, half, far)
        attend([chip], half, x == 0)
        attend([chip, chip3, chip4, chip5, chip6], half, far)
        met(chip0, half, uses0)
        met(chip1, half, uses1)
        met(chip2, half, uses2)
        attend([chip0], half, y == 1)
        attend([chip0, chip2], half, y == 2)
        attend([chip0, chip1, chip2], half, y == 3)

    pl.when(part == 1)(begin)
    collect(3)
    pl.when(part != 1)(begin)
    early(part3, True)
    tail(part2)
    own(rest)
    met(chip0, rest, uses0)
    met(chip3, rest, far)
    attend([chip], rest, (x == 0) & (y == 0))
    attend([chip, chip0], rest, (x == 0) & (y > 0))
    attend([chip, chip3], rest, far & (y == 0))
    attend([chip, chip0, chip3], rest, far & (y > 0))
    tail(part3, False)
    met(chip1, rest, uses1)
    met(chip2, rest, uses2)
    for which in (chip4, chip5, chip6):
        met(which, rest, far)
    attend([chip2], rest, (x == 0) & (y == 2))
    attend([chip1, chip2], rest, (x == 0) & (y == 3))
    attend([chip4, chip5, chip6], rest, far & (y < 2))
    attend([chip4, chip5, chip6, chip2], rest, far & (y == 2))
    attend([chip4, chip5, chip6, chip1, chip2], rest, far & (y == 3))

    loads[3].wait()
    loads[4].wait()
    level = noise[s]
    row = gate[pl.ds(level, 1), :]
    mixed = accum[...] / total[...]
    normed = mixed * lax.rsqrt(jnp.mean(mixed * mixed, axis=1, keepdims=True) + eps)
    for head in range(GROUP):
        lanes = slice(head * HEAD_WIDTH, (head + 1) * HEAD_WIDTH)
        block = normed[head * PEERS * RUN : (head + 1) * PEERS * RUN, :] * row[:, lanes]
        ready[:, :, lanes] = block.reshape(PEERS, RUN, HEAD_WIDTH).astype(jnp.bfloat16)
    pltpu.make_async_copy(ready.at[me], out.at[0, :, mine], out_recv).start()
    for step in range(1, PEERS):
        peer = fellow(step)
        copy = pltpu.make_async_remote_copy(
            src_ref=ready.at[peer],
            dst_ref=out.at[0, :, mine],
            send_sem=out_send.at[step],
            recv_sem=out_recv,
            device_id=(s, seat(peer, part)),
            device_id_type=MESH,
        )
        copy.start()
        sends.append((None, copy))

    for condition, copy in sends:
        if condition is None:
            copy.wait_send()
        else:
            pl.when(condition)(copy.wait_send)
    arrival(out, out_recv)


def body(*arrays):
    queries, key_value_pages, block_table, page_mask, noise_level, level_gate = arrays
    anywhere = pl.BlockSpec(memory_space=pl.ANY)
    dma = pltpu.SemaphoreType.DMA
    return pl.pallas_call(
        kernel,
        out_shape=jax.ShapeDtypeStruct(queries.shape, jnp.bfloat16),
        in_specs=[anywhere] * len(arrays),
        out_specs=anywhere,
        scratch_shapes=[
            pltpu.VMEM((SPANS, PARTS, 2, PEERS, RUN, HEAD_WIDTH), jnp.bfloat16),
            pltpu.VMEM((PEERS, RUN, WIDE), jnp.bfloat16),
            pltpu.VMEM((ROWS, HEAD_WIDTH), jnp.bfloat16),
            pltpu.VMEM((PEERS, RUN, WIDE), jnp.bfloat16),
            pltpu.VMEM((level_gate.shape[0], WIDE), jnp.float32),
            pltpu.VMEM(key_value_pages.shape[1:], jnp.bfloat16),
            pltpu.VMEM((KEY_VALUE_HEADS, 2, RUN, HEAD_WIDTH), jnp.bfloat16),
            pltpu.VMEM(block_table.shape, jnp.int32),
            pltpu.VMEM(page_mask.shape, jnp.int32),
            pltpu.SMEM(noise_level.shape, jnp.int32),
            pltpu.VMEM((SPANS // 2, PARTS, 8, 128), jnp.float32),
            pltpu.VMEM((ROWS, 1), jnp.float32),
            pltpu.VMEM((ROWS, 1), jnp.float32),
            pltpu.VMEM((ROWS, HEAD_WIDTH), jnp.float32),
            dma((5,)),
            pltpu.SemaphoreType.REGULAR((2,)),
            dma((2 * PEERS,)),
            dma((PARTS,)),
            dma((7,)),
            dma((PEERS,)),
            dma,
            dma((64,)),
            dma((SPANS, PARTS)),
            dma((32,)),
            dma((SPANS, PARTS)),
            dma((PEERS,)),
            dma,
        ],
        compiler_params=pltpu.CompilerParams(
            collective_id=0, has_side_effects=True, vmem_limit_bytes=16 * 1024 * 1024
        ),
    )(*(pltpu.with_memory_space_constraint(array, pltpu.HBM) for array in arrays))


def solution(mesh):
    in_specs = (P("section", "seq", None), P("section", "seq", None, None), P(), P(), P(), P())
    out_specs = P("section", "seq", None)
    return jax.shard_map(body, mesh=mesh, in_specs=in_specs, out_specs=out_specs, check_vma=False)
```

```python
import functools

import jax
import jax.numpy as jnp
from jax import lax
from jax.experimental import pallas as pl
from jax.experimental.pallas import tpu as pltpu
from jax.sharding import PartitionSpec as P

QUERY_HEADS = 32
KEY_VALUE_HEADS = 8
HEAD_WIDTH = 128
SPANS = 16
PAGES = 64
PARTS = 4
PEERS = 8
RUN = 8
GROUP = QUERY_HEADS // KEY_VALUE_HEADS
WIDE = GROUP * HEAD_WIDTH
ROWS = GROUP * PEERS * RUN
SPAN = PARTS * PEERS * RUN
EXPONENT = HEAD_WIDTH ** (-0.5) * 1.4426950408889634
HIDDEN = -3e30
MESH = pl.DeviceIdType.MESH

eps = 1e-06


def kernel(
    queries,
    pool,
    table_any,
    mask_any,
    noise_any,
    gates,
    out,
    kv,
    arrived,
    rows,
    ready,
    gate,
    raw,
    source,
    table,
    mask,
    noise,
    bias,
    top,
    total,
    accum,
    local_sem,
    ready_sem,
    spread_send,
    spread_recv,
    deep_send,
    query_send,
    query_recv,
    relay_send,
    relay_recv,
    share_send,
    share_recv,
    out_send,
    out_recv,
):
    s = lax.axis_index("section")
    t = lax.axis_index("seq")
    chip, core = s // 2, s % 2
    x, y = chip // 4, chip % 4
    column, z = t // 16, t % 16
    part = z // 4
    me = column * 4 + z % 4
    ahead, behind = column * 16 + (z + 4) % 16, column * 16 + (z + 12) % 16

    def fellow(step):
        turn = (0, 2, 1, 3, 2, 1, 3, 0)[step]
        side = (me // 4 + (0 if step in (0, 4, 5, 6) else 1)) % 2
        return side * 4 + (me + turn) % 4

    def seat(peer, block):
        return (peer // 4) * 16 + block * 4 + peer % 4

    def section(xx, yy):
        return (xx * 4 + yy) * 2 + core

    up, down = (y + 1) % 4, (y + 3) % 4
    partner = chip * 2 + 1 - core

    barrier = pltpu.get_barrier_semaphore()
    corner = section(1 - x, (y + 1 + 2 * x) % 4)
    flip = 1 - 2 * core
    cross = [other + flip for other in (section(x, up), section(x, down), corner)]
    for other in (section(x, up), section(x, down), section(1 - x, y), corner, partner, *cross):
        pl.semaphore_signal(barrier, inc=1, device_id=(other, t), device_id_type=MESH)
    for step in range(1, PEERS):
        pl.semaphore_signal(
            barrier, inc=1, device_id=(s, seat(fellow(step), part)), device_id_type=MESH
        )
    @pl.when(part == 0)
    def _():
        for block in range(1, PARTS):
            for peer in range(PEERS):
                pl.semaphore_signal(
                    barrier, inc=1, device_id=(s, seat(peer, block)), device_id_type=MESH
                )

    beside = jnp.where(part % 3 == 0, behind, ahead)

    @pl.when(part > 0)
    def _():
        pl.semaphore_signal(barrier, inc=1, device_id=(s, beside), device_id_type=MESH)

    mine = pl.ds(pl.multiple_of(me * WIDE, WIDE), WIDE)
    loads = [
        pltpu.make_async_copy(pool.at[0], raw, local_sem.at[0]),
        pltpu.make_async_copy(table_any, table, local_sem.at[1]),
        pltpu.make_async_copy(mask_any, mask, local_sem.at[2]),
        pltpu.make_async_copy(gates.at[:, mine], gate, local_sem.at[3]),
        pltpu.make_async_copy(noise_any, noise, local_sem.at[4]),
    ]
    for load in loads:
        load.start()

    loads[0].wait()
    for head in range(KEY_VALUE_HEADS):
        for kind in range(2):
            first = (kind * KEY_VALUE_HEADS + head) * HEAD_WIDTH
            for page in range(2):
                source[head, kind, page * 4 : (page + 1) * 4, :] = raw[
                    page, :, first : first + HEAD_WIDTH
                ]

    @pl.when(core == 0)
    def _():
        kv[s + 1] = jnp.zeros(kv.shape[1:], kv.dtype)

    top[...] = jnp.full(top.shape, -1e30, jnp.float32)
    total[...] = jnp.zeros(total.shape, jnp.float32)
    accum[...] = jnp.zeros(accum.shape, jnp.float32)

    inner = (part == 1) | (part == 2)
    extra = jnp.where(part == 2, 2, 0) + jnp.where(part == 3, 1, 0)
    pl.semaphore_wait(barrier, 15 + jnp.where(part > 0, PEERS, 0) + extra)

    @pl.when(inner)
    def _():
        pl.semaphore_signal(ready_sem.at[0], inc=1, device_id=(s, behind), device_id_type=MESH)

    @pl.when(part == 3)
    def _():
        pl.semaphore_signal(ready_sem.at[1], inc=1, device_id=(s, ahead), device_id_type=MESH)

    sends = []

    def spread(turn, step, block, condition, kind=None):
        peer = fellow(step)
        whole = kind is None
        copy = pltpu.make_async_remote_copy(
            src_ref=source.at[peer] if whole else source.at[peer, kind],
            dst_ref=kv.at[s, part, :, me] if whole else kv.at[s, part, kind, me],
            send_sem=spread_send.at[turn * PEERS + step],
            recv_sem=spread_recv.at[part],
            device_id=(s, seat(peer, block)),
            device_id_type=MESH,
        )
        pl.when(condition)(copy.start)
        sends.append((condition, copy))

    for step in range(PEERS):
        spread(1, step, 0, inner)
        spread(1, step, 0, part == 3, 0)
    pltpu.make_async_copy(source.at[me], kv.at[s, part, :, me], spread_recv.at[part]).start()
    for step in range(1, PEERS):
        spread(0, step, part, s >= 0)
    loads[1].wait()
    loads[2].wait()
    place = lax.broadcasted_iota(jnp.int32, (SPAN, PAGES), 0)
    holder = ((place // 32) % 2) * 16 + (place // 64) * 4 + (place // 8) % 4
    page = holder * 2 + (place % 8) // 4
    wanted = mask[pl.ds(s, 1), :].astype(jnp.float32)
    for c in range(SPANS):
        onehot = (table[c : c + 1, :] == page).astype(jnp.float32)
        row = jnp.broadcast_to(wanted[:, c * PAGES : (c + 1) * PAGES], (8, PAGES))
        seen = lax.dot_general(row, onehot, (((1,), (1,)), ((), ())))
        hide = jnp.where(seen > 0.5, 0.0, HIDDEN)
        lanes = slice((c % 2) * 64, (c % 2) * 64 + 64)
        for piece in range(PARTS):
            bias[c // 2, piece, :, lanes] = hide[:, piece * 64 : (piece + 1) * 64]

    def drain(copies):
        for condition, copy in copies:
            if condition is None:
                copy.wait_send()
            else:
                pl.when(condition)(copy.wait_send)

    count = [0, 0]

    def relay(slot, piece, other, condition, arrivals=None):
        arrivals = relay_recv if arrivals is None else arrivals
        copy = pltpu.make_async_remote_copy(
            src_ref=kv.at[slot, piece],
            dst_ref=kv.at[slot, piece],
            send_sem=relay_send.at[count[0]],
            recv_sem=arrivals.at[slot, piece],
            device_id=(other, t),
            device_id_type=MESH,
        )
        count[0] += 1
        pl.when(condition)(copy.start)
        sends.append((condition, copy))

    def share(slot, piece, condition):
        copy = pltpu.make_async_remote_copy(
            src_ref=kv.at[slot, piece],
            dst_ref=kv.at[slot, piece],
            send_sem=share_send.at[count[1]],
            recv_sem=share_recv.at[slot, piece],
            device_id=(partner, t),
            device_id_type=MESH,
        )
        count[1] += 1
        pl.when(condition)(copy.start)
        sends.append((condition, copy))

    def arrival(ref, sem):
        pltpu.make_async_copy(ref, ref, sem).wait()

    def landed(slot, piece, condition):
        @pl.when(condition)
        def _():
            arrival(kv.at[slot, piece], relay_recv.at[slot, piece])

    def attend(chunks, pieces, condition):
        @pl.when(condition)
        def _():
            scores, values = [], []
            for which in chunks:
                units = [(which * 2 + n, piece) for piece in pieces for n in range(2)]
                keys, value = (
                    jnp.concatenate(
                        [kv[a, b, kind].reshape(PEERS * RUN, HEAD_WIDTH) for a, b in units], axis=0
                    )
                    for kind in range(2)
                )
                hide = jnp.concatenate([bias[which, piece, 0:1, :] for piece in pieces], axis=1)
                score = lax.dot_general(
                    rows[...], keys, (((1,), (1,)), ((), ())), preferred_element_type=jnp.float32
                )
                scores.append(score + hide)
                values.append(value)
            before = top[...]
            peak = functools.reduce(jnp.maximum, scores)
            after = jnp.maximum(before, jnp.max(peak, axis=1, keepdims=True))
            shrink = jnp.exp2((before - after) * EXPONENT)
            weights = [jnp.exp2((score - after) * EXPONENT) for score in scores]
            top[...] = after
            mass = jnp.sum(functools.reduce(jnp.add, weights), axis=1, keepdims=True)
            total[...] = total[...] * shrink + mass
            update = accum[...] * shrink
            for weight, value in zip(weights, values):
                update += jnp.dot(
                    weight.astype(jnp.bfloat16), value, preferred_element_type=jnp.float32
                )
            accum[...] = update

    always = s >= 0
    far = x == 1

    others = [
        part,
        1 - part % 2,
        jnp.where(part == 2, 3, 2),
        jnp.where(part < 2, 3, part - 2),
    ]

    def deep(number, piece, other, condition, kind=None):
        ref = kv.at[s, piece] if kind is None else kv.at[s, piece, kind]
        copy = pltpu.make_async_remote_copy(
            src_ref=ref,
            dst_ref=ref,
            send_sem=deep_send.at[number],
            recv_sem=spread_recv.at[piece],
            device_id=(s, other),
            device_id_type=MESH,
        )
        pl.when(condition)(copy.start)
        sends.append((condition, copy))

    def collect(turn):
        piece = others[turn]
        arrival(kv.at[s, piece], spread_recv.at[piece])
        outward(piece)
        if turn == 0:
            deep(0, part, ahead, part == 2)
            deep(0, part, ahead, part == 3, 1)
            deep(1, part, behind, part >= 2)
        if turn == 1:
            deep(4, piece, beside, part < 2)
        if turn == 2:
            deep(5, piece, behind, part == 2, 0)
        if turn == 3:
            deep(6, piece, ahead, part == 0, 1)

    def twice(slot, piece, other, condition, double):
        relay(slot, piece, other, condition)
        if double:
            relay(slot, piece, other + flip, condition, share_recv)

    def outward(piece):
        relay(s, piece, section(x, up), (x == 0) | (y < 3))
        relay(s, piece, section(1, y), x == 0)
        relay(s, piece, section(x, down), y == 0)
        relay(s, piece, section(1, up), x == 0)
        share(s, piece, core == 0)

    chip0, chip1, chip2 = x * 4 + down, x * 4, x * 4 + (y + 2) % 4
    chip3, chip4, chip5, chip6 = y, down, up, (y + 2) % 4
    gets0, uses0, uses1, uses2 = (x == 0) | (y >= 1), y >= 1, y == 3, y >= 2

    def early(piece, double=False):
        slot = chip0 * 2 + core
        landed(slot, piece, gets0)
        twice(slot, piece, section(x, up), (y == 1) | (y == 2), double)
        twice(slot, piece, section(1, up), x == 0, double)
        share(slot, piece, uses0)
        slot = chip3 * 2 + core
        landed(slot, piece, far)
        twice(slot, piece, section(1, down), far, double)
        share(slot, piece, far)

    def late(piece, which, condition, passed=True):
        slot = which * 2 + core
        landed(slot, piece, condition)
        if passed:
            share(slot, piece, condition)

    def tail(piece, passed=True):
        late(piece, chip4, far)
        late(piece, chip1, uses1)
        late(piece, chip2, uses2, passed)
        late(piece, chip5, far, passed)
        late(piece, chip6, far, passed)

    def met(which, pieces, condition):
        slot = which * 2 + 1 - core
        for piece in pieces:

            @pl.when(condition)
            def _():
                arrival(kv.at[slot, piece], share_recv.at[slot, piece])

    def own(pieces):
        met(chip, pieces, core == 1)

    collect(0)
    for step in range(PEERS):
        peer = fellow(step)
        piece = queries.at[0, :, pl.ds(pl.multiple_of(peer * WIDE, WIDE), WIDE)]
        if step == 0:
            pltpu.make_async_copy(piece, arrived.at[me], query_recv).start()
            continue
        copy = pltpu.make_async_remote_copy(
            src_ref=piece,
            dst_ref=arrived.at[me],
            send_sem=query_send.at[step],
            recv_sem=query_recv,
            device_id=(s, seat(peer, part)),
            device_id_type=MESH,
        )
        copy.start()
        sends.append((None, copy))

    part0, part1, part2, part3 = others
    half, rest = (part0, part1), (part2, part3)
    @pl.when(part < 2)
    def _():
        pl.semaphore_wait(ready_sem.at[0], 1)

    deep(2, part, ahead, part < 2)
    early(part0)

    @pl.when(part == 0)
    def _():
        pl.semaphore_wait(ready_sem.at[1], 1)

    deep(3, part, behind, part == 0)
    collect(1)
    tail(part0)
    early(part1)
    started = len(sends)
    collect(2)
    arrival(arrived, query_recv)
    for head in range(GROUP):
        lanes = slice(head * HEAD_WIDTH, (head + 1) * HEAD_WIDTH)
        tall = arrived[:, :, lanes].astype(jnp.float32).reshape(PEERS * RUN, HEAD_WIDTH)
        rows[head * PEERS * RUN : (head + 1) * PEERS * RUN, :] = tall.astype(jnp.bfloat16)

    tail(part1)
    early(part2)

    def begin():
        own(half)
        for which in (chip3, chip4, chip5, chip6):
            met(which, half, far)
        attend([chip], half, x == 0)
        attend([chip, chip3, chip4, chip5, chip6], half, far)
        met(chip0, half, uses0)
        met(chip1, half, uses1)
        met(chip2, half, uses2)
        attend([chip0], half, y == 1)
        attend([chip0, chip2], half, y == 2)
        attend([chip0, chip1, chip2], half, y == 3)

    pl.when(part == 1)(begin)
    collect(3)
    pl.when(part != 1)(begin)
    early(part3, True)
    tail(part2)
    drain(sends[:started])
    own(rest)
    met(chip0, rest, uses0)
    met(chip3, rest, far)
    attend([chip], rest, (x == 0) & (y == 0))
    attend([chip, chip0], rest, (x == 0) & (y > 0))
    attend([chip, chip3], rest, far & (y == 0))
    attend([chip, chip0, chip3], rest, far & (y > 0))
    tail(part3, False)
    met(chip1, rest, uses1)
    met(chip2, rest, uses2)
    for which in (chip4, chip5, chip6):
        met(which, rest, far)
    attend([chip2], rest, (x == 0) & (y == 2))
    attend([chip1, chip2], rest, (x == 0) & (y == 3))
    attend([chip4, chip5, chip6], rest, far & (y < 2))
    attend([chip4, chip5, chip6, chip2], rest, far & (y == 2))
    attend([chip4, chip5, chip6, chip1, chip2], rest, far & (y == 3))

    loads[3].wait()
    loads[4].wait()
    level = noise[s]
    row = gate[pl.ds(level, 1), :]
    mixed = accum[...] / total[...]
    normed = mixed * lax.rsqrt(jnp.mean(mixed * mixed, axis=1, keepdims=True) + eps)
    for head in range(GROUP):
        lanes = slice(head * HEAD_WIDTH, (head + 1) * HEAD_WIDTH)
        block = normed[head * PEERS * RUN : (head + 1) * PEERS * RUN, :] * row[:, lanes]
        ready[:, :, lanes] = block.reshape(PEERS, RUN, HEAD_WIDTH).astype(jnp.bfloat16)
    pltpu.make_async_copy(ready.at[me], out.at[0, :, mine], out_recv).start()
    for step in range(1, PEERS):
        peer = fellow(step)
        copy = pltpu.make_async_remote_copy(
            src_ref=ready.at[peer],
            dst_ref=out.at[0, :, mine],
            send_sem=out_send.at[step],
            recv_sem=out_recv,
            device_id=(s, seat(peer, part)),
            device_id_type=MESH,
        )
        copy.start()
        sends.append((None, copy))

    drain(sends[started:])
    arrival(out, out_recv)


def body(*arrays):
    queries, key_value_pages, block_table, page_mask, noise_level, level_gate = arrays
    anywhere = pl.BlockSpec(memory_space=pl.ANY)
    dma = pltpu.SemaphoreType.DMA
    return pl.pallas_call(
        kernel,
        out_shape=jax.ShapeDtypeStruct(queries.shape, jnp.bfloat16),
        in_specs=[anywhere] * len(arrays),
        out_specs=anywhere,
        scratch_shapes=[
            pltpu.VMEM((SPANS, PARTS, 2, PEERS, RUN, HEAD_WIDTH), jnp.bfloat16),
            pltpu.VMEM((PEERS, RUN, WIDE), jnp.bfloat16),
            pltpu.VMEM((ROWS, HEAD_WIDTH), jnp.bfloat16),
            pltpu.VMEM((PEERS, RUN, WIDE), jnp.bfloat16),
            pltpu.VMEM((level_gate.shape[0], WIDE), jnp.float32),
            pltpu.VMEM(key_value_pages.shape[1:], jnp.bfloat16),
            pltpu.VMEM((KEY_VALUE_HEADS, 2, RUN, HEAD_WIDTH), jnp.bfloat16),
            pltpu.VMEM(block_table.shape, jnp.int32),
            pltpu.VMEM(page_mask.shape, jnp.int32),
            pltpu.SMEM(noise_level.shape, jnp.int32),
            pltpu.VMEM((SPANS // 2, PARTS, 8, 128), jnp.float32),
            pltpu.VMEM((ROWS, 1), jnp.float32),
            pltpu.VMEM((ROWS, 1), jnp.float32),
            pltpu.VMEM((ROWS, HEAD_WIDTH), jnp.float32),
            dma((5,)),
            pltpu.SemaphoreType.REGULAR((2,)),
            dma((2 * PEERS,)),
            dma((PARTS,)),
            dma((7,)),
            dma((PEERS,)),
            dma,
            dma((32,)),
            dma((SPANS, PARTS)),
            dma((32,)),
            dma((SPANS, PARTS)),
            dma((PEERS,)),
            dma,
        ],
        compiler_params=pltpu.CompilerParams(
            collective_id=0, has_side_effects=True, vmem_limit_bytes=16 * 1024 * 1024
        ),
    )(*(pltpu.with_memory_space_constraint(array, pltpu.HBM) for array in arrays))


def solution(mesh):
    in_specs = (P("section", "seq", None), P("section", "seq", None, None), P(), P(), P(), P())
    out_specs = P("section", "seq", None)
    return jax.shard_map(body, mesh=mesh, in_specs=in_specs, out_specs=out_specs, check_vma=False)
```
